128 devices in a mesh: row: 8 (over y, core), col: 16 (over x, z).
Axes of the slice: x: 4, y: 4, z: 4, core: 2. Of those that a mesh axis runs over, the one named last changes fastest.
Arguments:
- points: bfloat16 [262144, 512], P(('row', 'col')), may hold values from -6 to 6
- targets: float32 [262144, 256], P(('row', 'col'))
- plan: int32 [6], replicated, may hold values from 0 to 511
- block_inverse: float32 [6, 512, 512], replicated
Outputs:
- residual: float32 [262144, 256], P(('row', 'col'))
- block_steps: bfloat16 [6, 512, 256], replicated
- losses: float32 [6], replicated
The draws below stay inside these ranges and needn't reach their ends.
All inputs are finite; a program needn't handle non-finite values.
Results may differ from the reference program's by a relative error of at most 0.0062.
Values may be sent and summed in bfloat16 or wider, within the bound.
A program may use at most 64 MiB of HBM per device.

```python
import jax
import jax.numpy as jnp
from jax import lax

F = 512
K = 256
BLK = 512
ROUNDS = 6
N = 262144
NB = 512


def draw_targets(key, part):
    first, second = jax.random.split(key, 2)
    position = jnp.arange(N, dtype=jnp.float32) / max(N - 1, 1)
    rough = jax.random.uniform(second, (N, 1), jnp.float32, 0.5, 1.5)
    base = jax.random.normal(first, (N, K), jnp.float32)
    scale = jnp.power(3.0, 0.5 * position)
    return base * rough * scale[:, None]


def draw_block_inverse(key, part):
    first, second = jax.random.split(key)
    diagonal = jax.random.uniform(first, (ROUNDS, BLK), jnp.float32, 0.15, 0.45)
    centre = -0.28 / BLK
    off = jax.random.normal(second, (ROUNDS, BLK, BLK), jnp.float32) * (0.15 / BLK ** 0.5) + centre
    eye = jnp.eye(BLK, dtype=jnp.float32)
    return off * (1.0 - eye)[None] + diagonal[:, :, None] * eye[None]


def place_ends(drawn, key, least, high):
    spot = [jax.random.randint(jax.random.fold_in(key, axis), (), 0, length) for axis, length in enumerate(drawn.shape)]
    widest = drawn.shape.index(max(drawn.shape))
    neighbour = spot[:widest] + [(spot[widest] + 1) % drawn.shape[widest]] + spot[widest + 1:]
    return drawn.at[tuple(spot)].set(least).at[tuple(neighbour)].set(high)


def block_levels(stream_key, dims, cuts, least, high):
    factor_of = 1.0
    for dim, parts in cuts:
        steps = jax.random.uniform(jax.random.fold_in(jax.random.fold_in(stream_key, 6), dim), (parts,), jnp.float32, least / len(cuts), high / len(cuts))
        factor_of = factor_of * jnp.repeat(jnp.exp(steps), dims[dim] // parts).reshape((-1,) + (1,) * (len(dims) - 1 - dim))
    return factor_of


def bell_draw(stream_key, shape, width, most, cuts=(), kind=jnp.bfloat16):
    array = jax.random.normal(stream_key, shape, jnp.float32) * width
    if len(cuts) > 0:
        array = block_levels(stream_key, shape, cuts, -0.22, 0.18) * array
    return jnp.clip(array, min=-most, max=most).astype(kind)


def setup_inputs(seed: int = 0) -> dict:
    key_list = jax.random.split(jax.random.key(seed), 5)
    points = bell_draw(key_list[0], (N, F), 1.0, 6.0, ((0, 128),))
    targets = draw_targets(jax.random.fold_in(key_list[4], 71), 0)
    plan = place_ends(jax.random.randint(key_list[2], (ROUNDS,), 0, NB), jax.random.fold_in(key_list[2], 1), 0, NB - 1).astype(jnp.int32)
    block_inverse = draw_block_inverse(jax.random.fold_in(key_list[4], 71), 0)
    return dict(points=points, targets=targets, plan=plan, block_inverse=block_inverse)


RIDGE = 1.0


def reference(points, targets, plan, block_inverse):
    gamma = 2.0 / F
    sqnorm = jnp.sum(jnp.square(points.astype(jnp.float32)), axis=1)
    residual = targets
    group = min(N, 8192)
    losses = []
    updates = []
    for r in range(ROUNDS):
        start = (plan[r] * BLK).astype(jnp.int32)
        block_rows = lax.dynamic_slice_in_dim(residual, start, BLK, 0)
        step = jnp.dot(block_inverse[r], block_rows, precision=lax.Precision.HIGHEST)
        step_half = step.astype(jnp.bfloat16)
        block_points = lax.dynamic_slice_in_dim(points, start, BLK, 0)
        block_norm = lax.dynamic_slice_in_dim(sqnorm, start, BLK, 0)

        def update(args):
            pts, norms, res = args
            inner = lax.dot_general(pts, block_points, (((1,), (1,)), ((), ())), preferred_element_type=jnp.float32)
            kernel = jnp.exp(-gamma * (norms[:, None] + block_norm[None, :] - 2.0 * inner)).astype(jnp.bfloat16)
            return res - jnp.dot(kernel, step_half, preferred_element_type=jnp.float32)

        residual = lax.map(update, (points.reshape(N // group, group, F), sqnorm.reshape(N // group, group), residual.reshape(N // group, group, K))).reshape(N, K)
        block_rows = lax.dynamic_slice_in_dim(residual, start, BLK, 0)
        residual = lax.dynamic_update_slice_in_dim(residual, block_rows - RIDGE * step, start, 0)
        updates.append(step_half)
        losses.append(jnp.sum(residual * residual) / (N * K))
    return residual, jnp.stack(updates), jnp.stack(losses).astype(jnp.float32)
```

```python
import jax
import jax.numpy as jnp
from jax import lax
from jax.experimental import pallas as pl
from jax.experimental.pallas import tpu as pltpu
from jax.sharding import PartitionSpec as P

RIDGE = 1.0
MESH = pl.DeviceIdType.MESH
ROUNDS = 6
BLK = 512
F = 512
K = 256
GAMMA = 2.0 / F
NT = (((1,), (1,)), ((), ()))
NN = (((1,), (0,)), ((), ()))
COPIES = 19


def coords():
    row = lax.axis_index("row")
    col = lax.axis_index("col")
    return (lax.div(col, 4), lax.div(row, 2), lax.rem(col, 4), lax.rem(row, 2))


def device(x, y, z, core):
    return (y * 2 + core, x * 4 + z)


def shifted(me, axis, delta):
    c = list(me)
    c[axis] = lax.rem(c[axis] + delta, 4)
    return device(*c)


def owner_of(block):
    d = block >> 2
    row, col = d >> 4, d & 15
    return (col >> 2, row >> 1, col & 3, row & 1), block & 3


def pick(slots, index):
    low = lax.select_n(index == 1, slots[0], slots[1])
    high = lax.select_n(index == 3, slots[2], slots[3])
    return lax.select_n(index >= 2, low, high)


class Chunk:
    def __init__(self, index, r, me, plan_ref, src, dst, bufs, sems):
        self.i, self.r, self.me = index, r, me
        self.src, self.dst = src, dst
        self.snd, self.cb, self.s0, self.ra, self.rb, self.rl, self.rr, self.s1, self.b2, self.b3 = (
            b.at[r] for b in bufs
        )
        self.ss, self.rs = sems
        self.owner, self.blk = owner_of(plan_ref[r])
        color = index % 3
        self.ax = [(color + j) % 3 for j in range(3)]
        self.a, self.b, self.c = (me[t] for t in self.ax)
        self.oa, self.ob, self.oc = (self.owner[t] for t in self.ax)
        self.core, self.ocore = me[3], self.owner[3]
        self.copies = {}

    def send(self, k, src, dst, dev):
        c = pltpu.make_async_remote_copy(
            src_ref=src, dst_ref=dst, send_sem=self.ss.at[self.i, k], recv_sem=self.rs.at[self.i, k],
            device_id=dev, device_id_type=MESH,
        )
        c.start()
        self.copies[k] = c

    def got(self, *ks):
        for k in ks:
            self.copies[k].wait_recv()

    def partner(self):
        x, y, z, core = self.me
        return device(x, y, z, 1 - core)

    def step0(self):
        self.snd[...] = self.src[self.blk, pl.ds(pl.multiple_of((1 - self.core) * 256, 256), 256), :]
        self.send(0, self.snd, self.cb, self.partner())

    def step1(self):
        self.got(0)
        own = self.src[self.blk, pl.ds(pl.multiple_of(self.core * 256, 256), 256), :]
        self.s0[...] = lax.select_n(self.ocore == self.core, self.cb[...], own)
        opp = lax.rem(self.a + 2, 4) * 64
        self.send(1, self.s0.at[pl.ds(pl.multiple_of(opp, 64), 32)], self.ra, shifted(self.me, self.ax[0], 1))
        self.send(2, self.s0.at[pl.ds(pl.multiple_of(opp + 32, 32), 32)], self.rb, shifted(self.me, self.ax[0], 3))

    def step2(self):
        self.got(1, 2)
        right = pl.multiple_of(lax.rem(self.a + 1, 4) * 64, 64)
        left = pl.multiple_of(lax.rem(self.a + 3, 4) * 64, 64)
        d = (self.oa - self.a) & 3
        ra = self.s0.at[pl.ds(right, 32)]
        ra[...] = lax.select_n(d == 3, ra[...], self.ra[...])
        lb = self.s0.at[pl.ds(pl.multiple_of(left + 32, 32), 32)]
        lb[...] = lax.select_n(d == 1, lb[...], self.rb[...])
        self.send(3, self.s0.at[pl.ds(right, 64)], self.rl, shifted(self.me, self.ax[0], 1))
        self.send(4, self.s0.at[pl.ds(left, 64)], self.rr, shifted(self.me, self.ax[0], 3))

    def step3(self):
        self.got(3, 4)
        d = (self.oa - self.a) & 3
        mine = self.a * 64
        va = lax.select_n(d == 1, self.rl[0:32], self.rr[0:32])
        self.s1[0:32] = lax.select_n(d == 0, va, self.s0[pl.ds(pl.multiple_of(mine, 64), 32), :])
        vb = lax.select_n(d == 3, self.rr[32:64], self.rl[32:64])
        self.s1[32:64] = lax.select_n(d == 0, vb, self.s0[pl.ds(pl.multiple_of(mine + 32, 32), 32), :])
        self.b2[self.b] = self.s1[pl.ds(pl.multiple_of(self.b * 16, 16), 16), :]
        for t in (1, 2, 3):
            q = lax.rem(self.b + t, 4) * 16
            self.send(4 + t, self.s1.at[pl.ds(pl.multiple_of(q, 16), 16)], self.b2.at[self.b],
                      shifted(self.me, self.ax[1], t))

    def step4(self):
        self.got(5, 6, 7)
        self.b3[self.c] = pick(self.b2, self.ob)
        for t in (1, 2, 3):
            self.send(7 + t, self.b3.at[self.c], self.b3.at[self.c], shifted(self.me, self.ax[2], t))

    def rows(self, start, count):
        return self.dst.at[self.r, pl.ds(pl.multiple_of(self.core * 256 + start, min(count, 64)), count)]

    def step5(self):
        self.got(8, 9, 10)
        here = self.rows(self.a * 64 + self.b * 16, 16)
        here[...] = pick(self.b3, self.oc)
        for t in (1, 2, 3):
            self.send(10 + t, here, here, shifted(self.me, self.ax[1], t))

    def step6(self):
        self.got(11, 12, 13)
        here = self.rows(self.a * 64, 64)
        self.send(14, here, here, shifted(self.me, self.ax[0], 1))
        self.send(15, here, here, shifted(self.me, self.ax[0], 3))

    def step7(self):
        self.got(14, 15)
        fa = self.rows(lax.rem(self.a + 3, 4) * 64, 32)
        fb = self.rows(lax.rem(self.a + 1, 4) * 64 + 32, 32)
        self.send(16, fa, fa, shifted(self.me, self.ax[0], 1))
        self.send(17, fb, fb, shifted(self.me, self.ax[0], 3))

    def step8(self):
        self.got(16, 17)
        here = self.dst.at[self.r, pl.ds(pl.multiple_of(self.core * 256, 256), 256)]
        self.send(18, here, here, self.partner())

    def step9(self):
        self.got(18)

    def drain(self):
        for c in self.copies.values():
            c.wait_send()


STEPS = 10


def make_chunks(me, plan_ref, pts, tgt, outp, outt, bufp, buft, ss, rs):
    order = [("p", 0), ("p", 1), ("p", 2), ("p", 3), ("p", 4), ("p", 5),
             ("t", 0), ("t", 1), ("t", 2), ("t", 3), ("t", 4), ("t", 5)]
    chunks = []
    for i, (kind, r) in enumerate(order):
        if kind == "p":
            chunks.append(Chunk(i, r, me, plan_ref, pts, outp, bufp, (ss, rs)))
        else:
            chunks.append(Chunk(i, r, me, plan_ref, tgt, outt, buft, (ss, rs)))
    return chunks


def greet(peers):
    barrier = pltpu.get_barrier_semaphore()
    for dev in peers:
        pl.semaphore_signal(barrier, inc=1, device_id=dev, device_id_type=MESH)
    pl.semaphore_wait(barrier, len(peers))


def gather_kernel(plan_ref, pts, tgt, outp, outt, *scratch):
    bufp, buft, ss, rs = scratch[:10], scratch[10:20], scratch[20], scratch[21]
    me = coords()
    x, y, z, core = me
    greet([device(x, y, z, 1 - core)] + [shifted(me, ax, t) for ax in range(3) for t in (1, 2, 3)])
    chunks = make_chunks(me, plan_ref, pts, tgt, outp, outt, bufp, buft, ss, rs)
    batches = [chunks[3 * b:3 * b + 3] for b in range(4)]
    for tau in range(STEPS + 3):
        for b in range(4):
            s = tau - b
            if 0 <= s < STEPS:
                for ch in batches[b]:
                    getattr(ch, f"step{s}")()
    for ch in chunks:
        ch.drain()


def buffers(width, dtype):
    shapes = [(256,), (256,), (256,), (32,), (32,), (64,), (64,), (64,), (4, 16), (4, 16)]
    return [pltpu.VMEM((ROUNDS,) + s + (width,), dtype) for s in shapes]


def vm():
    return pl.BlockSpec(memory_space=pltpu.VMEM)


def sm():
    return pl.BlockSpec(memory_space=pltpu.SMEM)


def row_norm(block):
    sq = jnp.square(block.astype(jnp.float32))
    col = GAMMA * jnp.sum(sq, axis=1, keepdims=True)
    return col, jnp.transpose(jnp.broadcast_to(col, (block.shape[0], 128)))[0:1, :]


def kmat(x, xcol, b, brow):
    inner = lax.dot_general(x, b, NT, preferred_element_type=jnp.float32)
    return jnp.exp((2.0 * GAMMA) * inner - (xcol + brow)).astype(jnp.bfloat16)


def mm(a, b):
    return lax.dot_general(a, b, NN, preferred_element_type=jnp.float32)


def split(v):
    hi = v.astype(jnp.bfloat16)
    return hi, (v - hi.astype(jnp.float32)).astype(jnp.bfloat16)


def compute_kernel(plan_ref, pts, tgt, bp, bt, minv, res, steps_out, part, xcol, brow, bcol, steps):
    row = lax.axis_index("row")
    col = lax.axis_index("col")
    first = (row * 16 + col) * 4

    def norms(q, _):
        xcol[q] = row_norm(pts[q])[0]
        res[q] = tgt[q]
        return 0

    lax.fori_loop(0, 4, norms, 0)

    def block_norms(r, _):
        c, w = row_norm(bp[r])
        bcol[r] = c
        brow[r] = w
        return 0

    lax.fori_loop(0, ROUNDS, block_norms, 0)
    part[...] = jnp.zeros_like(part)

    def one_round(r, _):
        def earlier(s, y):
            k = kmat(bp[r], bcol[r], bp[s], brow[s])
            same = jnp.where(plan_ref[s] == plan_ref[r], RIDGE, 0.0)
            return y - mm(k, steps_out[s]) - same * steps[s]

        y = lax.fori_loop(0, r, earlier, bt[r])
        yh, yl = split(y)
        mh, ml = split(minv[r])
        step = mm(mh, yh) + (mm(mh, yl) + mm(ml, yh))
        steps[r] = step
        steps_out[r] = step.astype(jnp.bfloat16)

        def update(q, acc):
            k = kmat(pts[q], xcol[q], bp[r], brow[r])
            mine = jnp.where(plan_ref[r] == first + q, RIDGE, 0.0)
            new = res[q] - mm(k, steps_out[r]) - mine * steps[r]
            res[q] = new
            return acc + jnp.sum((new * new).reshape(64, 8, K), axis=0)

        acc = lax.fori_loop(0, 4, update, jnp.zeros((8, K), jnp.float32))
        part[r] = acc[:, :128] + acc[:, 128:]
        return 0

    lax.fori_loop(0, ROUNDS, one_round, 0)


def loss_kernel(total, part, out, mine, g1, mid, g2, ss1, rs1, ss2, rs2):
    me = coords()
    x, y, z, core = me
    near, far = [], []
    for t in range(1, 8):
        v = lax.rem(x * 2 + core + t, 8)
        near.append(device(lax.div(v, 2), y, z, lax.rem(v, 2)))
    for t in range(1, 16):
        v = lax.rem(y * 4 + z + t, 16)
        far.append(device(x, lax.div(v, 4), lax.rem(v, 4), core))
    greet(near + far)
    here1, here2 = x * 2 + core, y * 4 + z
    mine[...] = jnp.zeros_like(mine)
    for r in range(ROUNDS):
        mine[r:r + 1, :] = jnp.sum(part[r], axis=0, keepdims=True)
    g1[here1] = mine[...]
    c1 = []
    for t, dev in enumerate(near):
        c = pltpu.make_async_remote_copy(mine, g1.at[here1], ss1.at[t], rs1.at[t], device_id=dev, device_id_type=MESH)
        c.start()
        c1.append(c)
    for c in c1:
        c.wait_recv()
    mid[...] = jnp.sum(g1[...], axis=0)
    g2[here2] = mid[...]
    c2 = []
    for t, dev in enumerate(far):
        c = pltpu.make_async_remote_copy(mid, g2.at[here2], ss2.at[t], rs2.at[t], device_id=dev, device_id_type=MESH)
        c.start()
        c2.append(c)
    for c in c2:
        c.wait_recv()
    whole = jnp.sum(g2[...], axis=0)
    for r in range(ROUNDS):
        out[r] = jnp.sum(whole[r:r + 1, :]) * (1.0 / total)
    for c in c1 + c2:
        c.wait_send()


def on_device(points, targets, plan, block_inverse):
    rows = points.shape[0]
    total = rows * 128 * targets.shape[1]
    pts = points.reshape(4, BLK, F)
    tgt = targets.reshape(4, BLK, K)
    bp, bt = pl.pallas_call(
        gather_kernel,
        out_shape=(jax.ShapeDtypeStruct((ROUNDS, BLK, F), jnp.bfloat16),
                   jax.ShapeDtypeStruct((ROUNDS, BLK, K), jnp.float32)),
        in_specs=[sm(), vm(), vm()],
        out_specs=(vm(), vm()),
        scratch_shapes=buffers(F, jnp.bfloat16) + buffers(K, jnp.float32)
        + [pltpu.SemaphoreType.DMA((12, COPIES)), pltpu.SemaphoreType.DMA((12, COPIES))],
        compiler_params=pltpu.CompilerParams(collective_id=0, has_side_effects=True, vmem_limit_bytes=60 << 20),
        name="gather_blocks",
    )(plan, pts, tgt)
    res, steps, part = pl.pallas_call(
        compute_kernel,
        out_shape=(jax.ShapeDtypeStruct((4, BLK, K), jnp.float32),
                   jax.ShapeDtypeStruct((ROUNDS, BLK, K), jnp.bfloat16),
                   jax.ShapeDtypeStruct((ROUNDS, 8, 128), jnp.float32)),
        in_specs=[sm(), vm(), vm(), vm(), vm(), vm()],
        out_specs=(vm(), vm(), vm()),
        scratch_shapes=[pltpu.VMEM((4, BLK, 1), jnp.float32), pltpu.VMEM((ROUNDS, 1, BLK), jnp.float32),
                        pltpu.VMEM((ROUNDS, BLK, 1), jnp.float32), pltpu.VMEM((ROUNDS, BLK, K), jnp.float32)],
        compiler_params=pltpu.CompilerParams(vmem_limit_bytes=60 << 20),
        name="solve_update",
    )(plan, pts, tgt, bp, bt, block_inverse)
    losses = pl.pallas_call(
        lambda *a: loss_kernel(float(total), *a),
        out_shape=jax.ShapeDtypeStruct((ROUNDS,), jnp.float32),
        in_specs=[vm()],
        out_specs=sm(),
        scratch_shapes=[pltpu.VMEM((8, 128), jnp.float32), pltpu.VMEM((8, 8, 128), jnp.float32),
                        pltpu.VMEM((8, 128), jnp.float32), pltpu.VMEM((16, 8, 128), jnp.float32),
                        pltpu.SemaphoreType.DMA((7,)), pltpu.SemaphoreType.DMA((7,)),
                        pltpu.SemaphoreType.DMA((15,)), pltpu.SemaphoreType.DMA((15,))],
        compiler_params=pltpu.CompilerParams(collective_id=1, has_side_effects=True),
        name="sum_losses",
    )(part)
    return res.reshape(rows, K), steps, losses


def solution(mesh):
    placed = (P(("row", "col"), None), P(("row", "col"), None), P(), P())
    return jax.shard_map(
        on_device,
        mesh=mesh,
        in_specs=placed,
        out_specs=(P(("row", "col"), None), P(), P()),
        check_vma=False,
    )
```

```python
import jax
import jax.numpy as jnp
from jax import lax
from jax.experimental import pallas as pl
from jax.experimental.pallas import tpu as pltpu
from jax.sharding import PartitionSpec as P

RIDGE = 1.0
MESH = pl.DeviceIdType.MESH
ROUNDS = 6
BLK = 512
F = 512
K = 256
GAMMA = 2.0 / F
NT = (((1,), (1,)), ((), ()))
NN = (((1,), (0,)), ((), ()))
COPIES = 19
LOG2E = 1.4426950408889634


def coords():
    row = lax.axis_index("row")
    col = lax.axis_index("col")
    return (lax.div(col, 4), lax.div(row, 2), lax.rem(col, 4), lax.rem(row, 2))


def device(x, y, z, core):
    return (y * 2 + core, x * 4 + z)


def shifted(me, axis, delta):
    c = list(me)
    c[axis] = lax.rem(c[axis] + delta, 4)
    return device(*c)


def owner_of(block):
    d = block >> 2
    row, col = d >> 4, d & 15
    return (col >> 2, row >> 1, col & 3, row & 1), block & 3


def pick(slots, index):
    low = lax.select_n(index == 1, slots[0], slots[1])
    high = lax.select_n(index == 3, slots[2], slots[3])
    return lax.select_n(index >= 2, low, high)


class Chunk:
    def __init__(self, index, color, r, cols, me, plan_ref, src, dst, bufs, sems):
        self.i, self.r, self.me, self.cols = index, r, me, cols
        self.src, self.dst = src, dst
        snd, cb, s0, ra, rb, rl, rr, s1, b2, b3 = bufs
        self.snd, self.cb, self.s0, self.ra, self.rb, self.rl, self.rr, self.s1 = (
            b.at[r, :, cols] for b in (snd, cb, s0, ra, rb, rl, rr, s1)
        )
        self.b2, self.b3 = b2.at[r, :, :, cols], b3.at[r, :, :, cols]
        self.ss, self.rs = sems
        self.owner, self.blk = owner_of(plan_ref[r])
        self.ax = [(color + j) % 3 for j in range(3)]
        self.a, self.b, self.c = (me[t] for t in self.ax)
        self.oa, self.ob, self.oc = (self.owner[t] for t in self.ax)
        self.core, self.ocore = me[3], self.owner[3]
        self.copies = {}

    def send(self, k, src, dst, dev):
        c = pltpu.make_async_remote_copy(
            src_ref=src, dst_ref=dst, send_sem=self.ss.at[self.i, k], recv_sem=self.rs.at[self.i, k],
            device_id=dev, device_id_type=MESH,
        )
        c.start()
        self.copies[k] = c

    def got(self, *ks):
        for k in ks:
            self.copies[k].wait_recv()

    def partner(self):
        x, y, z, core = self.me
        return device(x, y, z, 1 - core)

    def half(self, core):
        return self.src[self.blk, pl.ds(pl.multiple_of(core * 256, 256), 256), self.cols]

    def step0(self):
        self.snd[...] = self.half(1 - self.core)
        self.send(0, self.snd, self.cb, self.partner())

    def step1(self):
        self.got(0)
        self.s0[...] = lax.select_n(self.ocore == self.core, self.cb[...], self.half(self.core))
        opp = lax.rem(self.a + 2, 4) * 64
        self.send(1, self.s0.at[pl.ds(pl.multiple_of(opp, 64), 32)], self.ra, shifted(self.me, self.ax[0], 1))
        self.send(2, self.s0.at[pl.ds(pl.multiple_of(opp + 32, 32), 32)], self.rb, shifted(self.me, self.ax[0], 3))

    def step2(self):
        self.got(1, 2)
        right = pl.multiple_of(lax.rem(self.a + 1, 4) * 64, 64)
        left = pl.multiple_of(lax.rem(self.a + 3, 4) * 64, 64)
        d = (self.oa - self.a) & 3
        ra = self.s0.at[pl.ds(right, 32)]
        ra[...] = lax.select_n(d == 3, ra[...], self.ra[...])
        lb = self.s0.at[pl.ds(pl.multiple_of(left + 32, 32), 32)]
        lb[...] = lax.select_n(d == 1, lb[...], self.rb[...])
        self.send(3, self.s0.at[pl.ds(right, 64)], self.rl, shifted(self.me, self.ax[0], 1))
        self.send(4, self.s0.at[pl.ds(left, 64)], self.rr, shifted(self.me, self.ax[0], 3))

    def step3(self):
        self.got(3, 4)
        d = (self.oa - self.a) & 3
        mine = self.a * 64
        va = lax.select_n(d == 1, self.rl[0:32], self.rr[0:32])
        self.s1[0:32] = lax.select_n(d == 0, va, self.s0[pl.ds(pl.multiple_of(mine, 64), 32), :])
        vb = lax.select_n(d == 3, self.rr[32:64], self.rl[32:64])
        self.s1[32:64] = lax.select_n(d == 0, vb, self.s0[pl.ds(pl.multiple_of(mine + 32, 32), 32), :])
        self.b2[self.b] = self.s1[pl.ds(pl.multiple_of(self.b * 16, 16), 16), :]
        for t in (1, 2, 3):
            q = lax.rem(self.b + t, 4) * 16
            self.send(4 + t, self.s1.at[pl.ds(pl.multiple_of(q, 16), 16)], self.b2.at[self.b],
                      shifted(self.me, self.ax[1], t))

    def step4(self):
        self.got(5, 6, 7)
        self.b3[self.c] = pick(self.b2, self.ob)
        for t in (1, 2, 3):
            self.send(7 + t, self.b3.at[self.c], self.b3.at[self.c], shifted(self.me, self.ax[2], t))

    def rows(self, start, count):
        return self.dst.at[self.r, pl.ds(pl.multiple_of(self.core * 256 + start, min(count, 64)), count), self.cols]

    def step5(self):
        self.got(8, 9, 10)
        here = self.rows(self.a * 64 + self.b * 16, 16)
        here[...] = pick(self.b3, self.oc)
        for t in (1, 2, 3):
            self.send(10 + t, here, here, shifted(self.me, self.ax[1], t))

    def step6(self):
        self.got(11, 12, 13)
        here = self.rows(self.a * 64, 64)
        self.send(14, here, here, shifted(self.me, self.ax[0], 1))
        self.send(15, here, here, shifted(self.me, self.ax[0], 3))

    def step7(self):
        self.got(14, 15)
        fa = self.rows(lax.rem(self.a + 3, 4) * 64, 32)
        fb = self.rows(lax.rem(self.a + 1, 4) * 64 + 32, 32)
        self.send(16, fa, fa, shifted(self.me, self.ax[0], 1))
        self.send(17, fb, fb, shifted(self.me, self.ax[0], 3))

    def step8(self):
        self.got(16, 17)
        here = self.rows(0, 256)
        self.send(18, here, here, self.partner())

    def step9(self):
        self.got(18)

    def drain(self):
        for c in self.copies.values():
            c.wait_send()


STEPS = 10
WHOLE = slice(None)
BATCHES = [
    [("p", 0, slice(0, 128)), ("p", 0, slice(128, 256)), ("p", 0, slice(256, 512))],
    [("p", 1, WHOLE), ("p", 2, WHOLE), ("p", 3, WHOLE)],
    [("p", 4, WHOLE), ("p", 5, WHOLE), ("t", 0, WHOLE)],
    [("t", 1, WHOLE), ("t", 2, WHOLE), ("t", 3, WHOLE)],
    [("t", 4, WHOLE), ("t", 5, WHOLE)],
]
CHUNKS = sum(len(b) for b in BATCHES)
WIRE = [1.7, 0.7, 1.4, 1.0, 1.0, 1.0, 1.4, 0.7, 1.7]
FLIGHT = [1.0, 2.7, 2.7, 2.7, 2.7, 2.7, 2.7, 2.7, 1.0]
ISSUE = [0.4, 0.4, 0.25, 0.2, 0.15, 0.15, 0.1, 0.1, 0.1, 0.05]


def plan_order(units):
    order, done, now = [], set(), 0.0
    free = {"core": 0.0, "ici": 0.0}
    following = [0] * len(BATCHES)
    ready = [0.0] * len(BATCHES)
    size = [0.5] + [1.0] * (len(BATCHES) - 1)
    left = dict(units)
    while True:
        steps = [(ready[b], b) for b in range(len(BATCHES)) if following[b] < STEPS]
        if not steps and not left:
            return order
        due = [(b, ready[b]) for _, b in steps if ready[b] <= now]
        if due:
            b = due[0][0]
            s = following[b]
            order.append(("step", b, s))
            now += ISSUE[s] * len(BATCHES[b]) / 3
            if s == STEPS - 1:
                done.update(("block", k, r) for k, r, _ in BATCHES[b])
            else:
                link = "core" if s in (0, 8) else "ici"
                start = max(now, free[link])
                free[link] = start + WIRE[s] * size[b]
                ready[b] = free[link] + FLIGHT[s]
            following[b] += 1
            continue
        name = next((n for n, (_, needs) in left.items() if all(d in done for d in needs)), None)
        if name is not None:
            order.append(name)
            now += left.pop(name)[0]
            done.add(name)
            continue
        now = min(t for t, _ in steps)


def work_units():
    units = {}
    for q in range(4):
        units[("xnorm", q)] = (0.3, [])
    for r in range(ROUNDS):
        units[("minv", r)] = (0.5, [])
    for r in range(ROUNDS):
        before = [("upd", r - 1)] if r else []
        units[("solve", r)] = (0.8 + 0.25 * r, [("block", "t", r), ("minv", r)]
                               + [("pair", r, s) for s in range(r)] + ([("solve", r - 1)] if r else []))
        units[("upd", r)] = (1.1, [("solve", r), ("own", r, 0), ("own", r, 1), ("block", "t", ROUNDS - 1)] + before)
    for r in range(ROUNDS):
        units[("bnorm", r)] = (0.4, [("block", "p", r)])
        for s in range(r):
            units[("pair", r, s)] = (0.4, [("bnorm", r), ("bnorm", s)])
        for h in range(2):
            units[("own", r, h)] = (0.75, [("bnorm", r), ("xnorm", 3)])
    return units


ORDER = plan_order(work_units())


def greet(peers):
    barrier = pltpu.get_barrier_semaphore()
    for dev in peers:
        pl.semaphore_signal(barrier, inc=1, device_id=dev, device_id_type=MESH)
    pl.semaphore_wait(barrier, len(peers))


def buffers(width, dtype):
    shapes = [(256,), (256,), (256,), (32,), (32,), (64,), (64,), (64,), (4, 16), (4, 16)]
    return [pltpu.VMEM((ROUNDS,) + s + (width,), dtype) for s in shapes]


def to_row(col):
    return jnp.transpose(jnp.broadcast_to(col, (col.shape[0], 128)))[0:1, :]


def norm(block):
    sq = jnp.square(block.astype(jnp.float32))
    return (GAMMA * LOG2E) * jnp.sum(sq, axis=1, keepdims=True)


def kmat(x, xcol, b, brow):
    inner = lax.dot_general(x, b, NT, preferred_element_type=jnp.float32)
    return jnp.exp2((2.0 * GAMMA * LOG2E) * inner - (xcol + brow)).astype(jnp.bfloat16)


def mm(a, b):
    return lax.dot_general(a, b, NN, preferred_element_type=jnp.float32)


def split(v):
    hi = v.astype(jnp.bfloat16)
    return hi, (v - hi.astype(jnp.float32)).astype(jnp.bfloat16)


def whole_kernel(total, plan_ref, pts_hbm, tgt_hbm, inv_hbm, res_hbm, steps_hbm, out, *scratch):
    bufp, buft = scratch[:10], scratch[10:20]
    (ss, rs, pts, res, bp, bt, minv, mh, ml, kown, kp1, kp2, kp3, kp4, kp5, xcol, bcol, brow, steps, sh, part,
     mine_loss, g1, mid, g2, ss1, rs1, ss2, rs2, local, msem, osem) = scratch[20:]
    kp = [None, kp1, kp2, kp3, kp4, kp5]
    me = coords()
    x, y, z, core = me
    first = (lax.axis_index("row") * 16 + lax.axis_index("col")) * 4
    loads = [pltpu.make_async_copy(pts_hbm, pts, local.at[0]), pltpu.make_async_copy(tgt_hbm, res, local.at[1])]
    for c in loads:
        c.start()
    fetch = [pltpu.make_async_copy(inv_hbm.at[r], minv.at[r % 2], msem.at[r]) for r in range(ROUNDS)]
    fetch[0].start()
    fetch[1].start()
    near, far, near_id, far_id = [], [], x * 2 + core, y * 4 + z
    for t in range(1, 8):
        v = lax.rem(near_id + t, 8)
        near.append(device(lax.div(v, 2), y, z, lax.rem(v, 2)))
    for t in range(1, 16):
        v = lax.rem(far_id + t, 16)
        far.append(device(x, lax.div(v, 4), lax.rem(v, 4), core))
    greet(near + far)
    for c in loads:
        c.wait()

    batches, index = [], 0
    for batch in BATCHES:
        made = []
        for color, (kind, r, cols) in enumerate(batch):
            src, dst, bufs = (pts, bp, bufp) if kind == "p" else (res, bt, buft)
            made.append(Chunk(index, color, r, cols, me, plan_ref, src, dst, bufs, (ss, rs)))
            index += 1
        batches.append(made)
    writes = []

    def do_minv(r):
        fetch[r].wait()
        mh[r], ml[r] = split(minv[r % 2])
        if r + 2 < ROUNDS:
            fetch[r + 2].start()

    def do_bnorm(r):
        c = norm(bp[r])
        bcol[r] = c
        brow[r] = to_row(c)

    def do_xnorm(q):
        xcol[q] = norm(pts[q])

    def do_pair(r, s):
        kp[r][:, s * BLK:(s + 1) * BLK] = kmat(bp[r], bcol[r], bp[s], brow[s])

    def do_own(r, h):
        def tile(q, _):
            kown[r, q] = kmat(pts[q], xcol[q], bp[r], brow[r])
            return 0

        lax.fori_loop(2 * h, 2 * h + 2, tile, 0)

    def do_solve(r):
        v = bt[r]
        for s in range(r):
            v = v - jnp.where(plan_ref[s] == plan_ref[r], RIDGE, 0.0) * steps[s]
        if r:
            v = v - mm(kp[r][...], sh[0:r * BLK, :])
        yh, yl = split(v)
        step = mm(mh[r], yh) + (mm(mh[r], yl) + mm(ml[r], yh))
        steps[r] = step
        sh[r * BLK:(r + 1) * BLK, :] = step.astype(jnp.bfloat16)

    def do_upd(r):
        def tile(q, acc):
            mine = jnp.where(plan_ref[r] == first + q, RIDGE, 0.0)
            new = res[q] - mm(kown[r, q], sh[r * BLK:(r + 1) * BLK, :]) - mine * steps[r]
            res[q] = new
            return acc + jnp.sum((new * new).reshape(64, 8, K), axis=0)

        acc = lax.fori_loop(0, 4, tile, jnp.zeros((8, K), jnp.float32))
        part[r:r + 1, :] = jnp.sum(acc[:, :128] + acc[:, 128:], axis=0, keepdims=True)
        c = pltpu.make_async_copy(sh.at[r * BLK:(r + 1) * BLK, :], steps_hbm.at[r], osem.at[r])
        c.start()
        writes.append(c)

    part[...] = jnp.zeros_like(part)
    todo = {"minv": do_minv, "bnorm": do_bnorm, "xnorm": do_xnorm, "pair": do_pair, "own": do_own,
            "solve": do_solve, "upd": do_upd}
    for item in ORDER:
        if item[0] == "step":
            for ch in batches[item[1]]:
                getattr(ch, f"step{item[2]}")()
        else:
            todo[item[0]](*item[1:])

    mine_loss[...] = part[...]
    g1[near_id] = part[...]
    c1 = []
    for t, dev in enumerate(near):
        c = pltpu.make_async_remote_copy(mine_loss, g1.at[near_id], ss1.at[t], rs1.at[t], device_id=dev, device_id_type=MESH)
        c.start()
        c1.append(c)
    c = pltpu.make_async_copy(res, res_hbm, osem.at[ROUNDS])
    c.start()
    writes.append(c)
    for c in c1:
        c.wait_recv()
    mid[...] = jnp.sum(g1[...], axis=0)
    g2[far_id] = mid[...]
    c2 = []
    for t, dev in enumerate(far):
        c = pltpu.make_async_remote_copy(mid, g2.at[far_id], ss2.at[t], rs2.at[t], device_id=dev, device_id_type=MESH)
        c.start()
        c2.append(c)
    for batch in batches:
        for ch in batch:
            ch.drain()
    for c in c2:
        c.wait_recv()
    whole = jnp.sum(g2[...], axis=0)
    for r in range(ROUNDS):
        out[r] = jnp.sum(whole[r:r + 1, :]) * (1.0 / total)
    for c in c1 + c2:
        c.wait_send()
    for c in writes:
        c.wait()


def on_device(points, targets, plan, block_inverse):
    rows = points.shape[0]
    total = float(rows * 128 * targets.shape[1])
    anywhere = pl.BlockSpec(memory_space=pl.ANY)
    smem = pl.BlockSpec(memory_space=pltpu.SMEM)
    f32, b16, dma = jnp.float32, jnp.bfloat16, pltpu.SemaphoreType.DMA
    res, steps, losses = pl.pallas_call(
        lambda *refs: whole_kernel(total, *refs),
        out_shape=(jax.ShapeDtypeStruct((4, BLK, K), f32), jax.ShapeDtypeStruct((ROUNDS, BLK, K), b16),
                   jax.ShapeDtypeStruct((ROUNDS,), f32)),
        in_specs=[smem, anywhere, anywhere, anywhere],
        out_specs=(anywhere, anywhere, smem),
        scratch_shapes=buffers(F, b16) + buffers(K, f32) + [
            dma((CHUNKS, COPIES)), dma((CHUNKS, COPIES)),
            pltpu.VMEM((4, BLK, F), b16), pltpu.VMEM((4, BLK, K), f32),
            pltpu.VMEM((ROUNDS, BLK, F), b16), pltpu.VMEM((ROUNDS, BLK, K), f32),
            pltpu.VMEM((2, BLK, BLK), f32), pltpu.VMEM((ROUNDS, BLK, BLK), b16), pltpu.VMEM((ROUNDS, BLK, BLK), b16),
            pltpu.VMEM((ROUNDS, 4, BLK, BLK), b16),
            *[pltpu.VMEM((BLK, r * BLK), b16) for r in range(1, ROUNDS)],
            pltpu.VMEM((4, BLK, 1), f32), pltpu.VMEM((ROUNDS, BLK, 1), f32), pltpu.VMEM((ROUNDS, 1, BLK), f32),
            pltpu.VMEM((ROUNDS, BLK, K), f32), pltpu.VMEM((ROUNDS * BLK, K), b16), pltpu.VMEM((8, 128), f32),
            pltpu.VMEM((8, 128), f32), pltpu.VMEM((8, 8, 128), f32), pltpu.VMEM((8, 128), f32),
            pltpu.VMEM((16, 8, 128), f32),
            dma((7,)), dma((7,)), dma((15,)), dma((15,)), dma((2,)), dma((ROUNDS,)), dma((ROUNDS + 1,)),
        ],
        compiler_params=pltpu.CompilerParams(collective_id=0, has_side_effects=True, vmem_limit_bytes=67043328),
        name="block_ridge",
    )(plan, points.reshape(4, BLK, F), targets.reshape(4, BLK, K), block_inverse)
    return res.reshape(rows, K), steps, losses


def solution(mesh):
    placed = (P(("row", "col"), None), P(("row", "col"), None), P(), P())
    return jax.shard_map(
        on_device,
        mesh=mesh,
        in_specs=placed,
        out_specs=(P(("row", "col"), None), P(), P()),
        check_vma=False,
    )
```

```python
import jax
import jax.numpy as jnp
from jax import lax
from jax.experimental import pallas as pl
from jax.experimental.pallas import tpu as pltpu
from jax.sharding import PartitionSpec as P

RIDGE = 1.0
MESH = pl.DeviceIdType.MESH
ROUNDS = 6
BLK = 512
F = 512
K = 256
GAMMA = 2.0 / F
NT = (((1,), (1,)), ((), ()))
NN = (((1,), (0,)), ((), ()))
LOG2E = 1.4426950408889634


def coords():
    row = lax.axis_index("row")
    col = lax.axis_index("col")
    return (lax.div(col, 4), lax.div(row, 2), lax.rem(col, 4), lax.rem(row, 2))


def device(x, y, z, core):
    return (y * 2 + core, x * 4 + z)


def shifted(me, axis, delta):
    c = list(me)
    c[axis] = lax.rem(c[axis] + delta, 4)
    return device(*c)


def owner_of(block):
    d = block >> 2
    row, col = d >> 4, d & 15
    return (col >> 2, row >> 1, col & 3, row & 1), block & 3


def pick(slots, index):
    low = lax.select_n(index == 1, slots[0], slots[1])
    high = lax.select_n(index == 3, slots[2], slots[3])
    return lax.select_n(index >= 2, low, high)


class Chunk:
    def __init__(self, color, r, cols, me, plan_ref, src, dst, bufs, sems):
        self.r, self.me, self.cols = r, me, cols
        self.src, self.dst = src, dst
        snd, cb, s0, b1, s1, b2, b3 = bufs
        self.snd, self.cb, self.s0, self.s1 = (b.at[r, :, cols] for b in (snd, cb, s0, s1))
        self.b1, self.b2, self.b3 = (b.at[r, :, :, cols] for b in (b1, b2, b3))
        self.ra, self.rb = self.b1.at[0, 0:32], self.b1.at[0, 32:64]
        self.rl, self.rr = self.b1.at[1], self.b1.at[2]
        self.ssem, self.rsem = sems
        self.owner, self.blk = owner_of(plan_ref[r])
        self.ax = [(color + j) % 3 for j in range(3)]
        self.a, self.b, self.c = (me[t] for t in self.ax)
        self.oa, self.ob, self.oc = (self.owner[t] for t in self.ax)
        self.core, self.ocore = me[3], self.owner[3]
        self.stage = 0

    def send(self, src, dst, dev):
        pltpu.make_async_remote_copy(
            src_ref=src, dst_ref=dst, send_sem=self.ssem, recv_sem=self.rsem.at[self.stage],
            device_id=dev, device_id_type=MESH,
        ).start()

    def partner(self):
        x, y, z, core = self.me
        return device(x, y, z, 1 - core)

    def half(self, core):
        return self.src[self.blk, pl.ds(pl.multiple_of(core * 256, 256), 256), self.cols]

    def stage_half(self):
        self.snd[...] = self.half(1 - self.core)

    def step0(self):
        self.send(self.snd, self.cb, self.partner())

    def step1(self):
        self.s0[...] = lax.select_n(self.ocore == self.core, self.cb[...], self.half(self.core))
        opp = lax.rem(self.a + 2, 4) * 64
        self.send(self.s0.at[pl.ds(pl.multiple_of(opp, 64), 32)], self.ra, shifted(self.me, self.ax[0], 1))
        self.send(self.s0.at[pl.ds(pl.multiple_of(opp + 32, 32), 32)], self.rb, shifted(self.me, self.ax[0], 3))

    def direct1(self):
        self.s0[...] = lax.select_n(self.ocore == self.core, self.cb[...], self.half(self.core))
        self.b1[self.a] = self.s0[pl.ds(pl.multiple_of(self.a * 64, 64), 64), :]
        for t in (1, 2, 3):
            q = pl.multiple_of(lax.rem(self.a + t, 4) * 64, 64)
            self.send(self.s0.at[pl.ds(q, 64)], self.b1.at[self.a], shifted(self.me, self.ax[0], t))

    def direct3(self):
        self.s1[...] = pick(self.b1, self.oa)
        self.spread()

    def direct6(self):
        here = self.rows(self.a * 64, 64)
        for t in (1, 2, 3):
            self.send(here, here, shifted(self.me, self.ax[0], t))

    def step2(self):
        right = pl.multiple_of(lax.rem(self.a + 1, 4) * 64, 64)
        left = pl.multiple_of(lax.rem(self.a + 3, 4) * 64, 64)
        d = (self.oa - self.a) & 3
        ra = self.s0.at[pl.ds(right, 32)]
        ra[...] = lax.select_n(d == 3, ra[...], self.ra[...])
        lb = self.s0.at[pl.ds(pl.multiple_of(left + 32, 32), 32)]
        lb[...] = lax.select_n(d == 1, lb[...], self.rb[...])
        self.send(self.s0.at[pl.ds(right, 64)], self.rl, shifted(self.me, self.ax[0], 1))
        self.send(self.s0.at[pl.ds(left, 64)], self.rr, shifted(self.me, self.ax[0], 3))

    def step3(self):
        d = (self.oa - self.a) & 3
        mine = self.a * 64
        va = lax.select_n(d == 1, self.rl[0:32], self.rr[0:32])
        self.s1[0:32] = lax.select_n(d == 0, va, self.s0[pl.ds(pl.multiple_of(mine, 64), 32), :])
        vb = lax.select_n(d == 3, self.rr[32:64], self.rl[32:64])
        self.s1[32:64] = lax.select_n(d == 0, vb, self.s0[pl.ds(pl.multiple_of(mine + 32, 32), 32), :])
        self.spread()

    def spread(self):
        self.b2[self.b] = self.s1[pl.ds(pl.multiple_of(self.b * 16, 16), 16), :]
        for t in (1, 2, 3):
            q = lax.rem(self.b + t, 4) * 16
            self.send(self.s1.at[pl.ds(pl.multiple_of(q, 16), 16)], self.b2.at[self.b],
                      shifted(self.me, self.ax[1], t))

    def step4(self):
        self.b3[self.c] = pick(self.b2, self.ob)
        for t in (1, 2, 3):
            self.send(self.b3.at[self.c], self.b3.at[self.c], shifted(self.me, self.ax[2], t))

    def rows(self, start, count):
        return self.dst.at[self.r, pl.ds(pl.multiple_of(self.core * 256 + start, min(count, 64)), count), self.cols]

    def step5(self):
        here = self.rows(self.a * 64 + self.b * 16, 16)
        here[...] = pick(self.b3, self.oc)
        for t in (1, 2, 3):
            self.send(here, here, shifted(self.me, self.ax[1], t))

    def step6(self):
        here = self.rows(self.a * 64, 64)
        self.send(here, here, shifted(self.me, self.ax[0], 1))
        self.send(here, here, shifted(self.me, self.ax[0], 3))

    def step7(self):
        fa = self.rows(lax.rem(self.a + 3, 4) * 64, 32)
        fb = self.rows(lax.rem(self.a + 1, 4) * 64 + 32, 32)
        self.send(fa, fa, shifted(self.me, self.ax[0], 1))
        self.send(fb, fb, shifted(self.me, self.ax[0], 3))

    def step8(self):
        here = self.rows(0, 256)
        self.send(here, here, self.partner())

    def step9(self):
        pass


WHOLE = slice(None)
RING = [("step0", 1.7, 1.0, 256), ("step1", 0.7, 2.7, 64), ("step2", 1.4, 2.7, 128), ("step3", 1.0, 2.7, 48),
        ("step4", 1.0, 2.7, 48), ("step5", 1.0, 2.7, 48), ("step6", 1.4, 2.7, 128), ("step7", 0.7, 2.7, 64),
        ("step8", 1.7, 1.0, 256), ("step9", 0.0, 0.0, 0)]
DIRECT = [("step0", 1.7, 1.0, 256), ("direct1", 4.1, 3.0, 192), ("direct3", 1.0, 2.7, 48), ("step4", 1.0, 2.7, 48),
          ("step5", 1.0, 2.7, 48), ("direct6", 4.1, 3.0, 192), ("step8", 1.7, 1.0, 256), ("step9", 0.0, 0.0, 0)]
BATCHES = [
    (RING, 1, [("p", 0, slice(0, 128)), ("p", 0, slice(128, 256)), ("p", 0, slice(256, 512))]),
    (RING, 3, [("p", 1, WHOLE), ("p", 2, WHOLE), ("p", 3, WHOLE)]),
    (RING, 3, [("p", 4, WHOLE), ("p", 5, WHOLE), ("t", 0, WHOLE)]),
    (RING, 3, [("t", 1, WHOLE), ("t", 2, WHOLE), ("t", 3, WHOLE)]),
    (RING, 2, [("t", 4, WHOLE), ("t", 5, WHOLE)]),
]
ISSUE = {"step0": 0.1, "step1": 0.4, "direct1": 0.5}


def plan_order(units):
    order, done, now = [], set(), 0.0
    free = {"core": 0.0, "ici": 0.0}
    following = [0] * len(BATCHES)
    ready = [0.0] * len(BATCHES)
    left = dict(units)
    while True:
        steps = [(ready[b], b) for b, (form, _, _) in enumerate(BATCHES) if following[b] < len(form)]
        if not steps and not left:
            return order
        due = [b for t, b in steps if t <= now]
        if due:
            b = due[0]
            form, size, entries = BATCHES[b]
            s = following[b]
            name, wire, flight, _ = form[s]
            order.append(("step", b, s))
            now += ISSUE.get(name, 0.15) * size / 3
            if s == len(form) - 1:
                done.update(("block", k, r) for k, r, _ in entries)
            else:
                link = "core" if name in ("step0", "step8") else "ici"
                free[link] = max(now, free[link]) + wire * size / 3
                ready[b] = free[link] + flight
            following[b] += 1
            continue
        name = next((n for n, (_, needs) in left.items() if all(d in done for d in needs)), None)
        if name is not None:
            order.append(name)
            now += left.pop(name)[0]
            done.add(name)
            continue
        now = min(t for t, _ in steps)


def work_units():
    units = {}
    for q in range(4):
        units[("xnorm", q)] = (0.3, [])
    for r in range(ROUNDS):
        units[("minv", r)] = (0.5, [])
    for r in range(ROUNDS):
        units[("solve", r)] = (0.8 + 0.15 * r, [("block", "t", r), ("minv", r)]
                               + [("pair", r, s) for s in range(r)] + ([("solve", r - 1)] if r else []))
        units[("upd", r)] = (0.9, [("solve", r), ("block", "t", ROUNDS - 1)] + [("own", r, q) for q in range(4)]
                             + ([("upd", r - 1)] if r else []))
    for r in range(ROUNDS):
        units[("bnorm", r)] = (0.3, [("block", "p", r)])
        for s in range(r):
            units[("pair", r, s)] = (0.3, [("bnorm", r), ("bnorm", s)])
        for q in range(4):
            units[("own", r, q)] = (0.3, [("bnorm", r), ("xnorm", q)])
    return units


ORDER = plan_order(work_units())


def buffers(width, dtype):
    shapes = [(256,), (256,), (256,), (4, 64), (64,), (4, 16), (4, 16)]
    return [pltpu.VMEM((ROUNDS,) + s + (width,), dtype) for s in shapes]


def to_row(col):
    return jnp.transpose(jnp.broadcast_to(col, (col.shape[0], 128)))[0:1, :]


def norm(block):
    sq = jnp.square(block.astype(jnp.float32))
    return (GAMMA * LOG2E) * jnp.sum(sq, axis=1, keepdims=True)


def kmat(x, xcol, b, brow):
    inner = lax.dot_general(x, b, NT, preferred_element_type=jnp.float32)
    return jnp.exp2((2.0 * GAMMA * LOG2E) * inner - (xcol + brow)).astype(jnp.bfloat16)


def mm(a, b):
    return lax.dot_general(a, b, NN, preferred_element_type=jnp.float32)


def split(v):
    hi = v.astype(jnp.bfloat16)
    return hi, (v - hi.astype(jnp.float32)).astype(jnp.bfloat16)


def whole_kernel(total, plan_ref, pts_hbm, tgt_hbm, inv_hbm, res_hbm, steps_hbm, out, *scratch):
    bufp, buft = scratch[:7], scratch[7:14]
    (ss, rs, pts, res, bp, bt, minv, mh, ml, kown, kp1, kp2, kp3, kp4, kp5, xcol, bcol, brow, steps, sh, part,
     mine_loss, g1, mid, g2, lsem, local, msem, osem) = scratch[14:]
    kp = [None, kp1, kp2, kp3, kp4, kp5]
    me = coords()
    x, y, z, core = me
    first = (lax.axis_index("row") * 16 + lax.axis_index("col")) * 4
    loads = [pltpu.make_async_copy(pts_hbm, pts, local.at[0]), pltpu.make_async_copy(tgt_hbm, res, local.at[1])]
    for c in loads:
        c.start()
    fetch = [pltpu.make_async_copy(inv_hbm.at[r], minv.at[r % 2], msem.at[r]) for r in range(ROUNDS)]
    fetch[0].start()
    fetch[1].start()
    near, far, near_id, far_id = [], [], x * 2 + core, y * 4 + z
    for t in range(1, 8):
        v = lax.rem(near_id + t, 8)
        near.append(device(lax.div(v, 2), y, z, lax.rem(v, 2)))
    for t in range(1, 16):
        v = lax.rem(far_id + t, 16)
        far.append(device(x, lax.div(v, 4), lax.rem(v, 4), core))
    peers = [device(x, y, z, 1 - core)] + [shifted(me, ax, t) for ax in range(3) for t in (1, 2, 3)]
    barrier = pltpu.get_barrier_semaphore()
    for dev in peers:
        pl.semaphore_signal(barrier, inc=1, device_id=dev, device_id_type=MESH)
    for c in loads:
        c.wait()

    batches = []
    for b, (_, _, entries) in enumerate(BATCHES):
        made = []
        for color, (kind, r, cols) in enumerate(entries):
            src, dst, bufs = (pts, bp, bufp) if kind == "p" else (res, bt, buft)
            made.append(Chunk(color, r, cols, me, plan_ref, src, dst, bufs, (ss.at[b], rs.at[b])))
            made[-1].stage_half()
        batches.append(made)
    pl.semaphore_wait(barrier, len(peers))

    def await_ref(ref, sem):
        pltpu.make_async_copy(ref, ref, sem).wait()

    def await_bytes(kib, sem):
        await_ref(kown.at[0:kib], sem)

    def comm_step(b, s):
        form, size, _ = BATCHES[b]
        if s:
            await_bytes(form[s - 1][3] * size, rs.at[b, s - 1])
        for ch in batches[b]:
            ch.stage = s
            getattr(ch, form[s][0])()

    writes = []

    def do_minv(r):
        fetch[r].wait()
        mh[r], ml[r] = split(minv[r % 2])
        if r + 2 < ROUNDS:
            fetch[r + 2].start()

    def do_bnorm(r):
        c = norm(bp[r])
        bcol[r] = c
        brow[r] = to_row(c)

    def do_xnorm(q):
        xcol[q] = norm(pts[q])

    def do_pair(r, s):
        kp[r][:, s * BLK:(s + 1) * BLK] = kmat(bp[r], bcol[r], bp[s], brow[s])

    def own_rows(r, q):
        start = (r * 4 + q) * BLK
        return slice(start, start + BLK)

    def do_own(r, q):
        kown[own_rows(r, q), :] = kmat(pts[q], xcol[q], bp[r], brow[r])

    def do_solve(r):
        v = bt[r]
        for s in range(r):
            v = v - jnp.where(plan_ref[s] == plan_ref[r], RIDGE, 0.0) * steps[s]
        if r:
            v = v - mm(kp[r][...], sh[0:r * BLK, :])
        yh, yl = split(v)
        step = mm(mh[r], yh) + (mm(mh[r], yl) + mm(ml[r], yh))
        steps[r] = step
        sh[r * BLK:(r + 1) * BLK, :] = step.astype(jnp.bfloat16)

    def do_upd(r):
        acc = jnp.zeros((8, K), jnp.float32)
        for q in range(4):
            mine = jnp.where(plan_ref[r] == first + q, RIDGE, 0.0)
            new = res[q] - mm(kown[own_rows(r, q), :], sh[r * BLK:(r + 1) * BLK, :]) - mine * steps[r]
            res[q] = new
            acc = acc + jnp.sum((new * new).reshape(64, 8, K), axis=0)
        part[r:r + 1, :] = jnp.sum(acc[:, :128] + acc[:, 128:], axis=0, keepdims=True)
        c = pltpu.make_async_copy(sh.at[r * BLK:(r + 1) * BLK, :], steps_hbm.at[r], osem.at[r])
        c.start()
        writes.append(c)

    part[...] = jnp.zeros_like(part)
    todo = {"minv": do_minv, "bnorm": do_bnorm, "xnorm": do_xnorm, "pair": do_pair, "own": do_own,
            "solve": do_solve, "upd": do_upd}
    for item in ORDER:
        if item[0] == "step":
            comm_step(*item[1:])
        else:
            todo[item[0]](*item[1:])

    mine_loss[...] = part[...]
    g1[near_id] = part[...]
    for dev in near:
        pltpu.make_async_remote_copy(mine_loss, g1.at[near_id], lsem.at[0], lsem.at[1], device_id=dev,
                                     device_id_type=MESH).start()
    c = pltpu.make_async_copy(res, res_hbm, osem.at[ROUNDS])
    c.start()
    writes.append(c)
    await_ref(g1.at[0:7], lsem.at[1])
    mid[...] = jnp.sum(g1[...], axis=0)
    g2[far_id] = mid[...]
    for dev in far:
        pltpu.make_async_remote_copy(mid, g2.at[far_id], lsem.at[2], lsem.at[3], device_id=dev,
                                     device_id_type=MESH).start()
    for b, (form, size, _) in enumerate(BATCHES):
        await_bytes(sum(f[3] for f in form) * size, ss.at[b])
    await_ref(g1.at[0:7], lsem.at[0])
    await_ref(g2.at[0:15], lsem.at[3])
    whole = jnp.sum(g2[...], axis=0)
    for r in range(ROUNDS):
        out[r] = jnp.sum(whole[r:r + 1, :]) * (1.0 / total)
    await_ref(g2.at[0:15], lsem.at[2])
    for c in writes:
        c.wait()


def on_device(points, targets, plan, block_inverse):
    rows = points.shape[0]
    total = float(rows * 128 * targets.shape[1])
    anywhere = pl.BlockSpec(memory_space=pl.ANY)
    smem = pl.BlockSpec(memory_space=pltpu.SMEM)
    f32, b16, dma = jnp.float32, jnp.bfloat16, pltpu.SemaphoreType.DMA
    res, steps, losses = pl.pallas_call(
        lambda *refs: whole_kernel(total, *refs),
        out_shape=(jax.ShapeDtypeStruct((4, BLK, K), f32), jax.ShapeDtypeStruct((ROUNDS, BLK, K), b16),
                   jax.ShapeDtypeStruct((ROUNDS,), f32)),
        in_specs=[smem, anywhere, anywhere, anywhere],
        out_specs=(anywhere, anywhere, smem),
        scratch_shapes=buffers(F, b16) + buffers(K, f32) + [
            dma((len(BATCHES),)), dma((len(BATCHES), 9)),
            pltpu.VMEM((4, BLK, F), b16), pltpu.VMEM((4, BLK, K), f32),
            pltpu.VMEM((ROUNDS, BLK, F), b16), pltpu.VMEM((ROUNDS, BLK, K), f32),
            pltpu.VMEM((2, BLK, BLK), f32), pltpu.VMEM((ROUNDS, BLK, BLK), b16), pltpu.VMEM((ROUNDS, BLK, BLK), b16),
            pltpu.VMEM((ROUNDS * 4 * BLK, BLK), b16),
            *[pltpu.VMEM((BLK, r * BLK), b16) for r in range(1, ROUNDS)],
            pltpu.VMEM((4, BLK, 1), f32), pltpu.VMEM((ROUNDS, BLK, 1), f32), pltpu.VMEM((ROUNDS, 1, BLK), f32),
            pltpu.VMEM((ROUNDS, BLK, K), f32), pltpu.VMEM((ROUNDS * BLK, K), b16), pltpu.VMEM((8, 128), f32),
            pltpu.VMEM((8, 128), f32), pltpu.VMEM((8, 8, 128), f32), pltpu.VMEM((8, 128), f32),
            pltpu.VMEM((16, 8, 128), f32),
            dma((4,)), dma((2,)), dma((ROUNDS,)), dma((ROUNDS + 1,)),
        ],
        compiler_params=pltpu.CompilerParams(collective_id=0, has_side_effects=True, vmem_limit_bytes=67043328),
        name="block_ridge",
    )(plan, points.reshape(4, BLK, F), targets.reshape(4, BLK, K), block_inverse)
    return res.reshape(rows, K), steps, losses


def solution(mesh):
    placed = (P(("row", "col"), None), P(("row", "col"), None), P(), P())
    return jax.shard_map(
        on_device,
        mesh=mesh,
        in_specs=placed,
        out_specs=(P(("row", "col"), None), P(), P()),
        check_vma=False,
    )
```

```python
import jax
import jax.numpy as jnp
from jax import lax
from jax.experimental import pallas as pl
from jax.experimental.pallas import tpu as pltpu
from jax.sharding import PartitionSpec as P

RIDGE = 1.0
MESH = pl.DeviceIdType.MESH
ROUNDS = 6
BLK = 512
F = 512
K = 256
GAMMA = 2.0 / F
NT = (((1,), (1,)), ((), ()))
NN = (((1,), (0,)), ((), ()))
LOG2E = 1.4426950408889634


def coords():
    row = lax.axis_index("row")
    col = lax.axis_index("col")
    return (lax.div(col, 4), lax.div(row, 2), lax.rem(col, 4), lax.rem(row, 2))


def device(x, y, z, core):
    return (y * 2 + core, x * 4 + z)


def shifted(me, axis, delta):
    c = list(me)
    c[axis] = lax.rem(c[axis] + delta, 4)
    return device(*c)


def owner_of(block):
    d = block >> 2
    row, col = d >> 4, d & 15
    return (col >> 2, row >> 1, col & 3, row & 1), block & 3


def pick(slots, index):
    low = lax.select_n(index == 1, slots[0], slots[1])
    high = lax.select_n(index == 3, slots[2], slots[3])
    return lax.select_n(index >= 2, low, high)


class Chunk:
    def __init__(self, color, r, cols, me, plan_ref, src, dst, bufs, sems):
        self.r, self.me, self.cols = r, me, cols
        self.src, self.dst = src, dst
        snd, cb, s0, b1, s1, b2, b3 = bufs
        self.snd, self.cb, self.s0, self.s1 = (b.at[r, :, cols] for b in (snd, cb, s0, s1))
        self.b1, self.b2, self.b3 = (b.at[r, :, :, cols] for b in (b1, b2, b3))
        self.ra, self.rb = self.b1.at[0, 0:32], self.b1.at[0, 32:64]
        self.rl, self.rr = self.b1.at[1], self.b1.at[2]
        self.ssem, self.rsem = sems
        self.owner, self.blk = owner_of(plan_ref[r])
        self.ax = [(color + j) % 3 for j in range(3)]
        self.a, self.b, self.c = (me[t] for t in self.ax)
        self.oa, self.ob, self.oc = (self.owner[t] for t in self.ax)
        self.core, self.ocore = me[3], self.owner[3]
        self.stage = 0

    def send(self, src, dst, dev):
        pltpu.make_async_remote_copy(
            src_ref=src, dst_ref=dst, send_sem=self.ssem, recv_sem=self.rsem.at[self.stage],
            device_id=dev, device_id_type=MESH,
        ).start()

    def partner(self):
        x, y, z, core = self.me
        return device(x, y, z, 1 - core)

    def half(self, core):
        return self.src[self.blk, pl.ds(pl.multiple_of(core * 256, 256), 256), self.cols]

    def stage_half(self):
        self.snd[...] = self.half(1 - self.core)

    def step0(self):
        self.send(self.snd, self.cb, self.partner())

    def step1(self):
        self.s0[...] = lax.select_n(self.ocore == self.core, self.cb[...], self.half(self.core))
        opp = lax.rem(self.a + 2, 4) * 64
        self.send(self.s0.at[pl.ds(pl.multiple_of(opp, 64), 32)], self.ra, shifted(self.me, self.ax[0], 1))
        self.send(self.s0.at[pl.ds(pl.multiple_of(opp + 32, 32), 32)], self.rb, shifted(self.me, self.ax[0], 3))

    def direct1(self):
        self.s0[...] = lax.select_n(self.ocore == self.core, self.cb[...], self.half(self.core))
        self.b1[self.a] = self.s0[pl.ds(pl.multiple_of(self.a * 64, 64), 64), :]
        for t in (1, 2, 3):
            q = pl.multiple_of(lax.rem(self.a + t, 4) * 64, 64)
            self.send(self.s0.at[pl.ds(q, 64)], self.b1.at[self.a], shifted(self.me, self.ax[0], t))

    def direct3(self):
        self.s1[...] = pick(self.b1, self.oa)
        self.spread()

    def direct6(self):
        here = self.rows(self.a * 64, 64)
        for t in (1, 2, 3):
            self.send(here, here, shifted(self.me, self.ax[0], t))

    def step2(self):
        right = pl.multiple_of(lax.rem(self.a + 1, 4) * 64, 64)
        left = pl.multiple_of(lax.rem(self.a + 3, 4) * 64, 64)
        d = (self.oa - self.a) & 3
        ra = self.s0.at[pl.ds(right, 32)]
        ra[...] = lax.select_n(d == 3, ra[...], self.ra[...])
        lb = self.s0.at[pl.ds(pl.multiple_of(left + 32, 32), 32)]
        lb[...] = lax.select_n(d == 1, lb[...], self.rb[...])
        self.send(self.s0.at[pl.ds(right, 64)], self.rl, shifted(self.me, self.ax[0], 1))
        self.send(self.s0.at[pl.ds(left, 64)], self.rr, shifted(self.me, self.ax[0], 3))

    def step3(self):
        d = (self.oa - self.a) & 3
        mine = self.a * 64
        va = lax.select_n(d == 1, self.rl[0:32], self.rr[0:32])
        self.s1[0:32] = lax.select_n(d == 0, va, self.s0[pl.ds(pl.multiple_of(mine, 64), 32), :])
        vb = lax.select_n(d == 3, self.rr[32:64], self.rl[32:64])
        self.s1[32:64] = lax.select_n(d == 0, vb, self.s0[pl.ds(pl.multiple_of(mine + 32, 32), 32), :])
        self.spread()

    def spread(self):
        self.b2[self.b] = self.s1[pl.ds(pl.multiple_of(self.b * 16, 16), 16), :]
        for t in (1, 2, 3):
            q = lax.rem(self.b + t, 4) * 16
            self.send(self.s1.at[pl.ds(pl.multiple_of(q, 16), 16)], self.b2.at[self.b],
                      shifted(self.me, self.ax[1], t))

    def step4(self):
        self.b3[self.c] = pick(self.b2, self.ob)
        for t in (1, 2, 3):
            self.send(self.b3.at[self.c], self.b3.at[self.c], shifted(self.me, self.ax[2], t))

    def rows(self, start, count):
        return self.dst.at[self.r, pl.ds(pl.multiple_of(self.core * 256 + start, min(count, 64)), count), self.cols]

    def step5(self):
        here = self.rows(self.a * 64 + self.b * 16, 16)
        here[...] = pick(self.b3, self.oc)
        for t in (1, 2, 3):
            self.send(here, here, shifted(self.me, self.ax[1], t))

    def step6(self):
        here = self.rows(self.a * 64, 64)
        self.send(here, here, shifted(self.me, self.ax[0], 1))
        self.send(here, here, shifted(self.me, self.ax[0], 3))

    def step7(self):
        fa = self.rows(lax.rem(self.a + 3, 4) * 64, 32)
        fb = self.rows(lax.rem(self.a + 1, 4) * 64 + 32, 32)
        self.send(fa, fa, shifted(self.me, self.ax[0], 1))
        self.send(fb, fb, shifted(self.me, self.ax[0], 3))

    def step8(self):
        here = self.rows(0, 256)
        self.send(here, here, self.partner())

    def step9(self):
        pass


WHOLE = slice(None)
RING = [("step0", 1.7, 1.0, 256), ("step1", 0.7, 2.7, 64), ("step2", 1.4, 2.7, 128), ("step3", 1.0, 2.7, 48),
        ("step4", 1.0, 2.7, 48), ("step5", 1.0, 2.7, 48), ("step6", 1.4, 2.7, 128), ("step7", 0.7, 2.7, 64),
        ("step8", 1.7, 1.0, 256), ("step9", 0.0, 0.0, 0)]
DIRECT = [("step0", 1.7, 1.0, 256), ("direct1", 4.1, 3.0, 192), ("direct3", 1.0, 2.7, 48), ("step4", 1.0, 2.7, 48),
          ("step5", 1.0, 2.7, 48), ("direct6", 4.1, 3.0, 192), ("step8", 1.7, 1.0, 256), ("step9", 0.0, 0.0, 0)]
BATCHES = [
    (DIRECT, 3, [("p", 0, WHOLE), ("p", 1, WHOLE), ("p", 2, WHOLE)]),
    (DIRECT, 3, [("p", 3, WHOLE), ("p", 4, WHOLE), ("p", 5, WHOLE)]),
    (RING, 3, [("t", 0, WHOLE), ("t", 1, WHOLE), ("t", 2, WHOLE)]),
    (RING, 3, [("t", 3, WHOLE), ("t", 4, WHOLE), ("t", 5, WHOLE)]),
]
ISSUE = {"step0": 0.1, "step1": 0.4, "direct1": 0.5}


def plan_order(units):
    order, done, now = [], set(), 0.0
    free = {"core": 0.0, "ici": 0.0}
    following = [0] * len(BATCHES)
    ready = [0.0] * len(BATCHES)
    left = dict(units)
    while True:
        steps = [(ready[b], b) for b, (form, _, _) in enumerate(BATCHES) if following[b] < len(form)]
        if not steps and not left:
            return order
        due = [b for t, b in steps if t <= now]
        if due:
            b = due[0]
            form, size, entries = BATCHES[b]
            s = following[b]
            name, wire, flight, _ = form[s]
            order.append(("step", b, s))
            now += ISSUE.get(name, 0.15) * size / 3
            if s == 1:
                done.update(("taken", k, r) for k, r, _ in entries)
            if s == len(form) - 1:
                done.update(("block", k, r) for k, r, _ in entries)
            else:
                link = "core" if name in ("step0", "step8") else "ici"
                free[link] = max(now, free[link]) + wire * size / 3
                ready[b] = free[link] + flight
            following[b] += 1
            continue
        name = next((n for n, (_, needs) in left.items() if all(d in done for d in needs)), None)
        if name is not None:
            order.append(name)
            now += left.pop(name)[0]
            done.add(name)
            continue
        now = min(t for t, _ in steps)


def grouped(order, units, most):
    out, size = [], 0.0
    for item in order:
        if item[0] == "step":
            out.append(item)
            continue
        us = units[item][0]
        if out and out[-1][0] == "group" and size + us <= most and out[-1][1][-1][0] != "solve":
            out[-1][1].append(item)
            size += us
        else:
            out.append(("group", [item]))
            size = us
    return out


def work_units():
    units = {}
    for q in range(4):
        units[("xnorm", q)] = (0.3, [])
    for r in range(ROUNDS):
        units[("minv", r)] = (0.5, [])
    for r in range(ROUNDS):
        units[("solve", r)] = (0.8 + 0.15 * r, [("block", "t", r), ("minv", r)]
                               + [("pair", r, s) for s in range(r)] + ([("solve", r - 1)] if r else []))
        units[("upd", r)] = (0.9, [("solve", r)] + [("own", r, h) for h in range(2)]
                             + [("taken", "t", t) for t in range(ROUNDS)]
                             + ([("upd", r - 1)] if r else []))
    for r in range(ROUNDS):
        units[("bnorm", r)] = (0.3, [("block", "p", r)])
        for s in range(r):
            units[("pair", r, s)] = (0.3, [("bnorm", r), ("bnorm", s)])
        for h in range(2):
            units[("own", r, h)] = (0.6, [("bnorm", r), ("xnorm", 3)])
    return units


ORDER = grouped(plan_order(work_units()), work_units(), 2.6)


def buffers(width, dtype):
    shapes = [(256,), (256,), (256,), (4, 64), (64,), (4, 16), (4, 16)]
    return [pltpu.VMEM((ROUNDS,) + s + (width,), dtype) for s in shapes]


def to_row(col):
    return jnp.transpose(jnp.broadcast_to(col, (col.shape[0], 128)))[0:1, :]


def norm(block):
    sq = jnp.square(block.astype(jnp.float32))
    return (GAMMA * LOG2E) * jnp.sum(sq, axis=1, keepdims=True)


def kmat(x, xcol, b, brow):
    inner = lax.dot_general(x, b, NT, preferred_element_type=jnp.float32)
    return jnp.exp2((2.0 * GAMMA * LOG2E) * inner - (xcol + brow)).astype(jnp.bfloat16)


def mm(a, b):
    return lax.dot_general(a, b, NN, preferred_element_type=jnp.float32)


def split(v):
    hi = v.astype(jnp.bfloat16)
    return hi, (v - hi.astype(jnp.float32)).astype(jnp.bfloat16)


def whole_kernel(total, plan_ref, pts_hbm, tgt_hbm, inv_hbm, res_hbm, steps_hbm, out, *scratch):
    bufp, buft = scratch[:7], scratch[7:14]
    (ss, rs, pts, res, bp, bt, minv, mhl, kown, kp1, kp2, kp3, kp4, kp5, xcol, bcol, brow, steps, sh, part,
     mine_loss, g1, mid, g2, lsem, local, msem, osem) = scratch[14:]
    kp = [None, kp1, kp2, kp3, kp4, kp5]
    me = coords()
    x, y, z, core = me
    first = (lax.axis_index("row") * 16 + lax.axis_index("col")) * 4
    loads = [pltpu.make_async_copy(pts_hbm, pts, local.at[0]), pltpu.make_async_copy(tgt_hbm, res, local.at[1])]
    for c in loads:
        c.start()
    fetch = [pltpu.make_async_copy(inv_hbm.at[r], minv.at[r % 2], msem.at[r]) for r in range(ROUNDS)]
    fetch[0].start()
    fetch[1].start()
    near, far, near_id, far_id = [], [], x * 2 + core, y * 4 + z
    for t in range(1, 8):
        v = lax.rem(near_id + t, 8)
        near.append(device(lax.div(v, 2), y, z, lax.rem(v, 2)))
    for t in range(1, 16):
        v = lax.rem(far_id + t, 16)
        far.append(device(x, lax.div(v, 4), lax.rem(v, 4), core))
    peers = [device(x, y, z, 1 - core)] + [shifted(me, ax, t) for ax in range(3) for t in (1, 2, 3)]
    barrier = pltpu.get_barrier_semaphore()
    for dev in peers:
        pl.semaphore_signal(barrier, inc=1, device_id=dev, device_id_type=MESH)
    for c in loads:
        c.wait()

    batches = []
    for b, (_, _, entries) in enumerate(BATCHES):
        made = []
        for color, (kind, r, cols) in enumerate(entries):
            src, dst, bufs = (pts, bp, bufp) if kind == "p" else (res, bt, buft)
            made.append(Chunk(color, r, cols, me, plan_ref, src, dst, bufs, (ss.at[b], rs.at[b])))
            made[-1].stage_half()
        batches.append(made)
    pl.semaphore_wait(barrier, len(peers))

    def await_ref(ref, sem):
        pltpu.make_async_copy(ref, ref, sem).wait()

    def await_bytes(kib, sem):
        await_ref(kown.at[0:kib], sem)

    def comm_step(b, s):
        form, size, _ = BATCHES[b]
        if s:
            await_bytes(form[s - 1][3] * size, rs.at[b, s - 1])
        for ch in batches[b]:
            ch.stage = s
            getattr(ch, form[s][0])()


    def write(r):
        return pltpu.make_async_copy(sh.at[r * BLK:(r + 1) * BLK, :], steps_hbm.at[r], osem.at[r])


    def do_minv(r):
        fetch[r].wait()
        mhl[r, 0:BLK], mhl[r, BLK:2 * BLK] = split(minv[r % 2])
        if r + 2 < ROUNDS:
            fetch[r + 2].start()

    def do_bnorm(r):
        c = norm(bp[r])
        bcol[r] = c
        brow[r] = to_row(c)

    def do_xnorm(q):
        xcol[q] = norm(pts[q])

    def do_pair(r, s):
        kp[r][:, s * BLK:(s + 1) * BLK] = kmat(bp[r], bcol[r], bp[s], brow[s])

    def do_own(r, h):
        start = (r * 4 + 2 * h) * BLK
        x2 = pts[2 * h:2 * h + 2].reshape(2 * BLK, F)
        c2 = xcol[2 * h:2 * h + 2].reshape(2 * BLK, 1)
        kown[start:start + 2 * BLK, :] = kmat(x2, c2, bp[r], brow[r])

    def do_solve(r):
        v = bt[r]
        for s in range(r):
            v = v - jnp.where(plan_ref[s] == plan_ref[r], RIDGE, 0.0) * steps[s]
        if r:
            v = v - mm(kp[r][...], sh[0:r * BLK, :])
        yh, yl = split(v)
        both = mm(mhl[r], yh)
        step = both[0:BLK] + (mm(mhl[r, 0:BLK], yl) + both[BLK:2 * BLK])
        steps[r] = step
        sh[r * BLK:(r + 1) * BLK, :] = step.astype(jnp.bfloat16)

    def do_upd(r):
        acc = jnp.zeros((8, K), jnp.float32)
        prod = mm(kown[r * 4 * BLK:(r + 1) * 4 * BLK, :], sh[r * BLK:(r + 1) * BLK, :])
        for q in range(4):
            mine = jnp.where(plan_ref[r] == first + q, RIDGE, 0.0)
            new = res[q] - prod[q * BLK:(q + 1) * BLK] - mine * steps[r]
            res[q] = new
            acc = acc + jnp.sum((new * new).reshape(64, 8, K), axis=0)
        part[r:r + 1, :] = jnp.sum(acc[:, :128] + acc[:, 128:], axis=0, keepdims=True)
        write(r).start()

    part[...] = jnp.zeros_like(part)
    todo = {"minv": do_minv, "bnorm": do_bnorm, "xnorm": do_xnorm, "pair": do_pair, "own": do_own,
            "solve": do_solve, "upd": do_upd}
    for item in ORDER:
        if item[0] == "step":
            comm_step(*item[1:])
        else:

            @pl.when(core >= 0)
            def _():
                for name in item[1]:
                    todo[name[0]](*name[1:])

    mine_loss[...] = part[...]
    g1[near_id] = part[...]
    for dev in near:
        pltpu.make_async_remote_copy(mine_loss, g1.at[near_id], lsem.at[0], lsem.at[1], device_id=dev,
                                     device_id_type=MESH).start()
    put = pltpu.make_async_copy(res, res_hbm, osem.at[ROUNDS])
    put.start()
    await_ref(g1.at[0:7], lsem.at[1])
    mid[...] = jnp.sum(g1[...], axis=0)
    g2[far_id] = mid[...]
    for dev in far:
        pltpu.make_async_remote_copy(mid, g2.at[far_id], lsem.at[2], lsem.at[3], device_id=dev,
                                     device_id_type=MESH).start()
    for b, (form, size, _) in enumerate(BATCHES):
        await_bytes(sum(f[3] for f in form) * size, ss.at[b])
    await_ref(g1.at[0:7], lsem.at[0])
    await_ref(g2.at[0:15], lsem.at[3])
    whole = jnp.sum(g2[...], axis=0)
    for r in range(ROUNDS):
        out[r] = jnp.sum(whole[r:r + 1, :]) * (1.0 / total)
    await_ref(g2.at[0:15], lsem.at[2])
    put.wait()
    for r in range(ROUNDS):
        write(r).wait()


def on_device(points, targets, plan, block_inverse):
    rows = points.shape[0]
    total = float(rows * 128 * targets.shape[1])
    anywhere = pl.BlockSpec(memory_space=pl.ANY)
    smem = pl.BlockSpec(memory_space=pltpu.SMEM)
    f32, b16, dma = jnp.float32, jnp.bfloat16, pltpu.SemaphoreType.DMA
    res, steps, losses = pl.pallas_call(
        lambda *refs: whole_kernel(total, *refs),
        out_shape=(jax.ShapeDtypeStruct((4, BLK, K), f32), jax.ShapeDtypeStruct((ROUNDS, BLK, K), b16),
                   jax.ShapeDtypeStruct((ROUNDS,), f32)),
        in_specs=[smem, anywhere, anywhere, anywhere],
        out_specs=(anywhere, anywhere, smem),
        scratch_shapes=buffers(F, b16) + buffers(K, f32) + [
            dma((len(BATCHES),)), dma((len(BATCHES), 9)),
            pltpu.VMEM((4, BLK, F), b16), pltpu.VMEM((4, BLK, K), f32),
            pltpu.VMEM((ROUNDS, BLK, F), b16), pltpu.VMEM((ROUNDS, BLK, K), f32),
            pltpu.VMEM((2, BLK, BLK), f32), pltpu.VMEM((ROUNDS, 2 * BLK, BLK), b16),
            pltpu.VMEM((ROUNDS * 4 * BLK, BLK), b16),
            *[pltpu.VMEM((BLK, r * BLK), b16) for r in range(1, ROUNDS)],
            pltpu.VMEM((4, BLK, 1), f32), pltpu.VMEM((ROUNDS, BLK, 1), f32), pltpu.VMEM((ROUNDS, 1, BLK), f32),
            pltpu.VMEM((ROUNDS, BLK, K), f32), pltpu.VMEM((ROUNDS * BLK, K), b16), pltpu.VMEM((8, 128), f32),
            pltpu.VMEM((8, 128), f32), pltpu.VMEM((8, 8, 128), f32), pltpu.VMEM((8, 128), f32),
            pltpu.VMEM((16, 8, 128), f32),
            dma((4,)), dma((2,)), dma((ROUNDS,)), dma((ROUNDS + 1,)),
        ],
        compiler_params=pltpu.CompilerParams(collective_id=0, has_side_effects=True, vmem_limit_bytes=67043328),
        name="block_ridge",
    )(plan, points.reshape(4, BLK, F), targets.reshape(4, BLK, K), block_inverse)
    return res.reshape(rows, K), steps, losses


def solution(mesh):
    placed = (P(("row", "col"), None), P(("row", "col"), None), P(), P())
    return jax.shard_map(
        on_device,
        mesh=mesh,
        in_specs=placed,
        out_specs=(P(("row", "col"), None), P(), P()),
        check_vma=False,
    )
```

```python
import jax
import jax.numpy as jnp
from jax import lax
from jax.experimental import pallas as pl
from jax.experimental.pallas import tpu as pltpu
from jax.sharding import PartitionSpec as P

RIDGE = 1.0
MESH = pl.DeviceIdType.MESH
ROUNDS = 6
BLK = 512
F = 512
K = 256
GAMMA = 2.0 / F
NT = (((1,), (1,)), ((), ()))
NN = (((1,), (0,)), ((), ()))
LOG2E = 1.4426950408889634


def coords():
    row = lax.axis_index("row")
    col = lax.axis_index("col")
    return (lax.div(col, 4), lax.div(row, 2), lax.rem(col, 4), lax.rem(row, 2))


def device(x, y, z, core):
    return (y * 2 + core, x * 4 + z)


def shifted(me, axis, delta):
    c = list(me)
    c[axis] = lax.rem(c[axis] + delta, 4)
    return device(*c)


def owner_of(block):
    d = block >> 2
    row, col = d >> 4, d & 15
    return (col >> 2, row >> 1, col & 3, row & 1), block & 3


def pick(slots, index):
    low = lax.select_n(index == 1, slots[0], slots[1])
    high = lax.select_n(index == 3, slots[2], slots[3])
    return lax.select_n(index >= 2, low, high)


class Chunk:
    def __init__(self, color, r, cols, me, plan_ref, src, dst, bufs, sems):
        self.r, self.me, self.cols = r, me, cols
        self.src, self.dst = src, dst
        snd, cb, s0, b1, s1, b2, b3 = bufs
        self.snd, self.cb, self.s0, self.s1 = (b.at[r, :, cols] for b in (snd, cb, s0, s1))
        self.b1, self.b2, self.b3 = (b.at[r, :, :, cols] for b in (b1, b2, b3))
        self.ra, self.rb = self.b1.at[0, 0:32], self.b1.at[0, 32:64]
        self.rl, self.rr = self.b1.at[1], self.b1.at[2]
        self.ssem, self.rsem = sems
        self.owner, self.blk = owner_of(plan_ref[r])
        self.ax = [(color + j) % 3 for j in range(3)]
        self.a, self.b, self.c = (me[t] for t in self.ax)
        self.oa, self.ob, self.oc = (self.owner[t] for t in self.ax)
        self.core, self.ocore = me[3], self.owner[3]
        self.stage = 0

    def send(self, src, dst, dev):
        pltpu.make_async_remote_copy(
            src_ref=src, dst_ref=dst, send_sem=self.ssem, recv_sem=self.rsem.at[self.stage],
            device_id=dev, device_id_type=MESH,
        ).start()

    def partner(self):
        x, y, z, core = self.me
        return device(x, y, z, 1 - core)

    def half(self, core):
        return self.src[self.blk, pl.ds(pl.multiple_of(core * 256, 256), 256), self.cols]

    def stage_half(self):
        self.snd[...] = self.half(1 - self.core)

    def step0(self):
        self.send(self.snd, self.cb, self.partner())

    def step1(self):
        self.s0[...] = lax.select_n(self.ocore == self.core, self.cb[...], self.half(self.core))
        opp = lax.rem(self.a + 2, 4) * 64
        self.send(self.s0.at[pl.ds(pl.multiple_of(opp, 64), 32)], self.ra, shifted(self.me, self.ax[0], 1))
        self.send(self.s0.at[pl.ds(pl.multiple_of(opp + 32, 32), 32)], self.rb, shifted(self.me, self.ax[0], 3))

    def direct1(self):
        self.s0[...] = lax.select_n(self.ocore == self.core, self.cb[...], self.half(self.core))
        self.b1[self.a] = self.s0[pl.ds(pl.multiple_of(self.a * 64, 64), 64), :]
        for t in (1, 2, 3):
            q = pl.multiple_of(lax.rem(self.a + t, 4) * 64, 64)
            self.send(self.s0.at[pl.ds(q, 64)], self.b1.at[self.a], shifted(self.me, self.ax[0], t))

    def direct3(self):
        self.s1[...] = pick(self.b1, self.oa)
        self.spread()

    def direct6(self):
        here = self.rows(self.a * 64, 64)
        for t in (1, 2, 3):
            self.send(here, here, shifted(self.me, self.ax[0], t))

    def step2(self):
        right = pl.multiple_of(lax.rem(self.a + 1, 4) * 64, 64)
        left = pl.multiple_of(lax.rem(self.a + 3, 4) * 64, 64)
        d = (self.oa - self.a) & 3
        ra = self.s0.at[pl.ds(right, 32)]
        ra[...] = lax.select_n(d == 3, ra[...], self.ra[...])
        lb = self.s0.at[pl.ds(pl.multiple_of(left + 32, 32), 32)]
        lb[...] = lax.select_n(d == 1, lb[...], self.rb[...])
        self.send(self.s0.at[pl.ds(right, 64)], self.rl, shifted(self.me, self.ax[0], 1))
        self.send(self.s0.at[pl.ds(left, 64)], self.rr, shifted(self.me, self.ax[0], 3))

    def step3(self):
        d = (self.oa - self.a) & 3
        mine = self.a * 64
        va = lax.select_n(d == 1, self.rl[0:32], self.rr[0:32])
        self.s1[0:32] = lax.select_n(d == 0, va, self.s0[pl.ds(pl.multiple_of(mine, 64), 32), :])
        vb = lax.select_n(d == 3, self.rr[32:64], self.rl[32:64])
        self.s1[32:64] = lax.select_n(d == 0, vb, self.s0[pl.ds(pl.multiple_of(mine + 32, 32), 32), :])
        self.spread()

    def spread(self):
        self.b2[self.b] = self.s1[pl.ds(pl.multiple_of(self.b * 16, 16), 16), :]
        for t in (1, 2, 3):
            q = lax.rem(self.b + t, 4) * 16
            self.send(self.s1.at[pl.ds(pl.multiple_of(q, 16), 16)], self.b2.at[self.b],
                      shifted(self.me, self.ax[1], t))

    def step4(self):
        self.b3[self.c] = pick(self.b2, self.ob)
        for t in (1, 2, 3):
            self.send(self.b3.at[self.c], self.b3.at[self.c], shifted(self.me, self.ax[2], t))

    def rows(self, start, count):
        return self.dst.at[self.r, pl.ds(pl.multiple_of(self.core * 256 + start, min(count, 64)), count), self.cols]

    def step5(self):
        here = self.rows(self.a * 64 + self.b * 16, 16)
        here[...] = pick(self.b3, self.oc)
        for t in (1, 2, 3):
            self.send(here, here, shifted(self.me, self.ax[1], t))

    def step6(self):
        here = self.rows(self.a * 64, 64)
        self.send(here, here, shifted(self.me, self.ax[0], 1))
        self.send(here, here, shifted(self.me, self.ax[0], 3))

    def step7(self):
        fa = self.rows(lax.rem(self.a + 3, 4) * 64, 32)
        fb = self.rows(lax.rem(self.a + 1, 4) * 64 + 32, 32)
        self.send(fa, fa, shifted(self.me, self.ax[0], 1))
        self.send(fb, fb, shifted(self.me, self.ax[0], 3))

    def step8(self):
        here = self.rows(0, 256)
        self.send(here, here, self.partner())

    def step9(self):
        pass


WHOLE = slice(None)
RING = [("step0", 1.7, 1.0, 256), ("step1", 0.7, 2.7, 64), ("step2", 1.4, 2.7, 128), ("step3", 1.0, 2.7, 48),
        ("step4", 1.0, 2.7, 48), ("step5", 1.0, 2.7, 48), ("step6", 1.4, 2.7, 128), ("step7", 0.7, 2.7, 64),
        ("step8", 1.7, 1.0, 256), ("step9", 0.0, 0.0, 0)]
DIRECT = [("step0", 1.7, 1.0, 256), ("direct1", 4.1, 3.0, 192), ("direct3", 1.0, 2.7, 48), ("step4", 1.0, 2.7, 48),
          ("step5", 1.0, 2.7, 48), ("direct6", 4.1, 3.0, 192), ("step8", 1.7, 1.0, 256), ("step9", 0.0, 0.0, 0)]
BATCHES = [
    (DIRECT, 3, [("p", 0, WHOLE), ("p", 1, WHOLE), ("p", 2, WHOLE)]),
    (DIRECT, 3, [("p", 3, WHOLE), ("p", 4, WHOLE), ("p", 5, WHOLE)]),
    (RING, 3, [("t", 0, WHOLE), ("t", 1, WHOLE), ("t", 2, WHOLE)]),
    (RING, 3, [("t", 3, WHOLE), ("t", 4, WHOLE), ("t", 5, WHOLE)]),
]
ISSUE = {"step0": 0.1, "step1": 0.4, "direct1": 0.5}


def plan_order(units):
    order, done, now = [], set(), 0.0
    free = {"core": 0.0, "ici": 0.0}
    following = [0] * len(BATCHES)
    ready = [0.0] * len(BATCHES)
    left = dict(units)
    while True:
        steps = [(ready[b], b) for b, (form, _, _) in enumerate(BATCHES) if following[b] < len(form)]
        if not steps and not left:
            return order
        due = [b for t, b in steps if t <= now]
        if due:
            b = due[0]
            form, size, entries = BATCHES[b]
            s = following[b]
            name, wire, flight, _ = form[s]
            order.append(("step", b, s))
            now += ISSUE.get(name, 0.15) * size / 3
            if s == 1:
                done.update(("taken", k, r) for k, r, _ in entries)
            if s == len(form) - 1:
                done.update(("block", k, r) for k, r, _ in entries)
            else:
                link = "core" if name in ("step0", "step8") else "ici"
                free[link] = max(now, free[link]) + wire * size / 3
                ready[b] = free[link] + flight
            following[b] += 1
            continue
        name = next((n for n, (_, needs) in left.items() if all(d in done for d in needs)), None)
        if name is not None:
            order.append(name)
            now += left.pop(name)[0]
            done.add(name)
            continue
        now = min(t for t, _ in steps)


def grouped(order, units, most):
    out, size = [], 0.0
    for item in order:
        if item[0] == "step":
            out.append(item)
            continue
        us = units[item][0]
        if out and out[-1][0] == "group" and size + us <= most and out[-1][1][-1][0] != "solve":
            out[-1][1].append(item)
            size += us
        else:
            out.append(("group", [item]))
            size = us
    return out


def work_units():
    units = {}
    for q in range(4):
        units[("xnorm", q)] = (0.3, [])
    for r in range(ROUNDS):
        units[("minv", r)] = (0.5, [])
    for r in range(ROUNDS):
        units[("solve", r)] = (0.8 + 0.15 * r, [("block", "t", r), ("minv", r)]
                               + [("pair", r, s) for s in range(r)] + ([("solve", r - 1)] if r else []))
        units[("upd", r)] = (0.9, [("solve", r)] + [("own", r, h) for h in range(2)]
                             + [("taken", "t", t) for t in range(ROUNDS)]
                             + ([("upd", r - 1)] if r else []))
    for r in range(ROUNDS):
        units[("bnorm", r)] = (0.3, [("block", "p", r)])
        for s in range(r):
            units[("pair", r, s)] = (0.3, [("bnorm", r), ("bnorm", s)])
        for h in range(2):
            units[("own", r, h)] = (0.6, [("bnorm", r), ("xnorm", 3)])
    return units


ORDER = grouped(plan_order(work_units()), work_units(), 2.6)


def buffers(width, dtype):
    shapes = [(256,), (256,), (256,), (4, 64), (64,), (4, 16), (4, 16)]
    return [pltpu.VMEM((ROUNDS,) + s + (width,), dtype) for s in shapes]


def to_row(col):
    return jnp.transpose(jnp.broadcast_to(col, (col.shape[0], 128)))[0:1, :]


def norm(block):
    sq = jnp.square(block.astype(jnp.float32))
    return (GAMMA * LOG2E) * jnp.sum(sq, axis=1, keepdims=True)


def kmat(x, xcol, b, brow):
    inner = lax.dot_general(x, b, NT, preferred_element_type=jnp.float32)
    return jnp.exp2((2.0 * GAMMA * LOG2E) * inner - (xcol + brow)).astype(jnp.bfloat16)


def mm(a, b):
    return lax.dot_general(a, b, NN, preferred_element_type=jnp.float32)


def split(v):
    hi = v.astype(jnp.bfloat16)
    return hi, (v - hi.astype(jnp.float32)).astype(jnp.bfloat16)


def whole_kernel(total, plan_ref, pts_hbm, tgt_hbm, inv_hbm, res_hbm, steps_hbm, out, *scratch):
    bufp, buft = scratch[:7], scratch[7:14]
    (ss, rs, pts, res, bp, bt, minv, mhl, kown, kp1, kp2, kp3, kp4, kp5, xcol, bcol, brow, steps, sh, part,
     mine_loss, g1, mid, g2, lsem, local, msem, osem) = scratch[14:]
    kp = [None, kp1, kp2, kp3, kp4, kp5]
    me = coords()
    x, y, z, core = me
    first = (lax.axis_index("row") * 16 + lax.axis_index("col")) * 4
    loads = [pltpu.make_async_copy(pts_hbm, pts, local.at[0]), pltpu.make_async_copy(tgt_hbm, res, local.at[1])]
    for c in loads:
        c.start()
    fetch = [pltpu.make_async_copy(inv_hbm.at[r], minv.at[r % 2], msem.at[r]) for r in range(ROUNDS)]
    fetch[0].start()
    fetch[1].start()
    near, far, near_id, far_id = [], [], x * 2 + core, y * 4 + z
    for t in range(1, 8):
        v = lax.rem(near_id + t, 8)
        near.append(device(lax.div(v, 2), y, z, lax.rem(v, 2)))
    for t in range(1, 16):
        v = lax.rem(far_id + t, 16)
        far.append(device(x, lax.div(v, 4), lax.rem(v, 4), core))
    peers = [device(x, y, z, 1 - core)] + [shifted(me, ax, t) for ax in range(3) for t in (1, 2, 3)]
    barrier = pltpu.get_barrier_semaphore()
    for dev in peers:
        pl.semaphore_signal(barrier, inc=1, device_id=dev, device_id_type=MESH)
    for c in loads:
        c.wait()

    batches = []
    for b, (_, _, entries) in enumerate(BATCHES):
        made = []
        for color, (kind, r, cols) in enumerate(entries):
            src, dst, bufs = (pts, bp, bufp) if kind == "p" else (res, bt, buft)
            made.append(Chunk(color, r, cols, me, plan_ref, src, dst, bufs, (ss.at[b], rs.at[b])))
            made[-1].stage_half()
        batches.append(made)
    pl.semaphore_wait(barrier, len(peers))

    def await_ref(ref, sem):
        pltpu.make_async_copy(ref, ref, sem).wait()

    def await_bytes(kib, sem):
        await_ref(kown.at[0:kib], sem)

    def comm_step(b, s):
        form, size, _ = BATCHES[b]
        if s:
            await_bytes(form[s - 1][3] * size, rs.at[b, s - 1])
        for ch in batches[b]:
            ch.stage = s
            getattr(ch, form[s][0])()


    def write(r):
        return pltpu.make_async_copy(sh.at[r * BLK:(r + 1) * BLK, :], steps_hbm.at[r], osem.at[r])


    def do_minv(r):
        fetch[r].wait()
        mhl[r, 0:BLK], mhl[r, BLK:2 * BLK] = split(minv[r % 2])
        if r + 2 < ROUNDS:
            fetch[r + 2].start()

    def do_bnorm(r):
        c = norm(bp[r])
        bcol[r] = c
        brow[r] = to_row(c)

    def do_xnorm(q):
        xcol[q] = norm(pts[q])

    def do_pair(r, s):
        kp[r][:, s * BLK:(s + 1) * BLK] = kmat(bp[r], bcol[r], bp[s], brow[s])

    def do_own(r, h):
        start = (r * 4 + 2 * h) * BLK
        x2 = pts[2 * h:2 * h + 2].reshape(2 * BLK, F)
        c2 = xcol[2 * h:2 * h + 2].reshape(2 * BLK, 1)
        kown[start:start + 2 * BLK, :] = kmat(x2, c2, bp[r], brow[r])

    def do_solve(r):
        v = bt[r]
        for s in range(r):
            v = v - jnp.where(plan_ref[s] == plan_ref[r], RIDGE, 0.0) * steps[s]
        if r:
            v = v - mm(kp[r][...], sh[0:r * BLK, :])
        yh, yl = split(v)
        both = mm(mhl[r], yh)
        step = both[0:BLK] + (mm(mhl[r, 0:BLK], yl) + both[BLK:2 * BLK])
        steps[r] = step
        sh[r * BLK:(r + 1) * BLK, :] = step.astype(jnp.bfloat16)

    def do_upd(r):
        acc = jnp.zeros((8, K), jnp.float32)
        prod = mm(kown[r * 4 * BLK:(r + 1) * 4 * BLK, :], sh[r * BLK:(r + 1) * BLK, :])
        for q in range(4):
            mine = jnp.where(plan_ref[r] == first + q, RIDGE, 0.0)
            new = res[q] - prod[q * BLK:(q + 1) * BLK] - mine * steps[r]
            res[q] = new
            acc = acc + jnp.sum((new * new).reshape(64, 8, K), axis=0)
        part[r:r + 1, :] = jnp.sum(acc[:, :128] + acc[:, 128:], axis=0, keepdims=True)
        write(r).start()

    part[...] = jnp.zeros_like(part)
    todo = {"minv": do_minv, "bnorm": do_bnorm, "xnorm": do_xnorm, "pair": do_pair, "own": do_own,
            "solve": do_solve, "upd": do_upd}
    for item in ORDER:
        if item[0] == "step":
            comm_step(*item[1:])
        else:

            @pl.when(core >= 0)
            def _():
                for name in item[1]:
                    todo[name[0]](*name[1:])

    mine_loss[...] = part[...]
    g1[near_id] = part[...]
    for dev in near:
        pltpu.make_async_remote_copy(mine_loss, g1.at[near_id], lsem.at[0], lsem.at[1], device_id=dev,
                                     device_id_type=MESH).start()
    put = pltpu.make_async_copy(res, res_hbm, osem.at[ROUNDS])
    put.start()
    await_ref(g1.at[0:7], lsem.at[1])
    mid[...] = jnp.sum(g1[...], axis=0)
    g2[far_id] = mid[...]
    for dev in far:
        pltpu.make_async_remote_copy(mid, g2.at[far_id], lsem.at[2], lsem.at[3], device_id=dev,
                                     device_id_type=MESH).start()
    for b, (form, size, _) in enumerate(BATCHES):
        await_bytes(sum(f[3] for f in form) * size, ss.at[b])
    await_ref(g1.at[0:7], lsem.at[0])
    await_ref(g2.at[0:15], lsem.at[3])
    whole = jnp.sum(g2[...], axis=0)
    for r in range(ROUNDS):
        out[r] = jnp.sum(whole[r:r + 1, :]) * (1.0 / total)
    await_ref(g2.at[0:15], lsem.at[2])
    put.wait()
    for r in range(ROUNDS):
        write(r).wait()


def put_kernel(res, steps, losses, res_out, steps_out, losses_out, res_vmem, steps_vmem, sem):
    moves = []
    for q in range(4):
        moves.append((pltpu.make_async_copy(res.at[q], res_vmem.at[q], sem.at[q]),
                      pltpu.make_async_copy(res_vmem.at[q], res_out.at[q], sem.at[q])))
    for q in range(3):
        two = pl.ds(2 * q, 2)
        moves.append((pltpu.make_async_copy(steps.at[two], steps_vmem.at[two], sem.at[4 + q]),
                      pltpu.make_async_copy(steps_vmem.at[two], steps_out.at[two], sem.at[4 + q])))
    for take, _ in moves:
        take.start()
    for r in range(ROUNDS):
        losses_out[r] = losses[r]
    for take, give in moves:
        take.wait()
        give.start()
    for _, give in moves:
        give.wait()


def on_device(points, targets, plan, block_inverse):
    rows = points.shape[0]
    total = float(rows * 128 * targets.shape[1])
    anywhere = pl.BlockSpec(memory_space=pl.ANY)
    smem = pl.BlockSpec(memory_space=pltpu.SMEM)
    f32, b16, dma = jnp.float32, jnp.bfloat16, pltpu.SemaphoreType.DMA
    res, steps, losses = pl.pallas_call(
        lambda *refs: whole_kernel(total, *refs),
        out_shape=(jax.ShapeDtypeStruct((4, BLK, K), f32), jax.ShapeDtypeStruct((ROUNDS, BLK, K), b16),
                   jax.ShapeDtypeStruct((ROUNDS,), f32)),
        in_specs=[smem, anywhere, anywhere, anywhere],
        out_specs=(anywhere, anywhere, smem),
        scratch_shapes=buffers(F, b16) + buffers(K, f32) + [
            dma((len(BATCHES),)), dma((len(BATCHES), 9)),
            pltpu.VMEM((4, BLK, F), b16), pltpu.VMEM((4, BLK, K), f32),
            pltpu.VMEM((ROUNDS, BLK, F), b16), pltpu.VMEM((ROUNDS, BLK, K), f32),
            pltpu.VMEM((2, BLK, BLK), f32), pltpu.VMEM((ROUNDS, 2 * BLK, BLK), b16),
            pltpu.VMEM((ROUNDS * 4 * BLK, BLK), b16),
            *[pltpu.VMEM((BLK, r * BLK), b16) for r in range(1, ROUNDS)],
            pltpu.VMEM((4, BLK, 1), f32), pltpu.VMEM((ROUNDS, BLK, 1), f32), pltpu.VMEM((ROUNDS, 1, BLK), f32),
            pltpu.VMEM((ROUNDS, BLK, K), f32), pltpu.VMEM((ROUNDS * BLK, K), b16), pltpu.VMEM((8, 128), f32),
            pltpu.VMEM((8, 128), f32), pltpu.VMEM((8, 8, 128), f32), pltpu.VMEM((8, 128), f32),
            pltpu.VMEM((16, 8, 128), f32),
            dma((4,)), dma((2,)), dma((ROUNDS,)), dma((ROUNDS + 1,)),
        ],
        compiler_params=pltpu.CompilerParams(collective_id=0, has_side_effects=True, vmem_limit_bytes=67043328),
        name="block_ridge",
    )(plan, points.reshape(4, BLK, F), targets.reshape(4, BLK, K), block_inverse)
    res, steps, losses = pl.pallas_call(
        put_kernel,
        out_shape=(jax.ShapeDtypeStruct((4, BLK, K), f32), jax.ShapeDtypeStruct((ROUNDS, BLK, K), b16),
                   jax.ShapeDtypeStruct((ROUNDS,), f32)),
        in_specs=[anywhere, anywhere, smem],
        out_specs=(anywhere, anywhere, smem),
        scratch_shapes=[pltpu.VMEM((4, BLK, K), f32), pltpu.VMEM((ROUNDS, BLK, K), b16), dma((7,))],
        name="put_results",
    )(res, steps, losses)
    return res.reshape(rows, K), steps, losses


def solution(mesh):
    placed = (P(("row", "col"), None), P(("row", "col"), None), P(), P())
    return jax.shard_map(
        on_device,
        mesh=mesh,
        in_specs=placed,
        out_specs=(P(("row", "col"), None), P(), P()),
        check_vma=False,
    )
```
